128 devices in a mesh: row: 8 (over y, core), col: 16 (over z, x).
Axes of the slice: x: 4, y: 4, z: 4, core: 2. Of those that a mesh axis runs over, the one named last changes fastest.
Arguments:
- features: bfloat16 [16, 2097152], P(None, ('row', 'col')), may hold values from -6 to 6
- point_weights: bfloat16 [8, 2097152], P(None, ('row', 'col')), may hold values from 0.049804688 to 1
- point_corner: int32 [2097152], P(('row', 'col')), may hold values from 0 to 342
- block_owner: int32 [16384, 1], P(('row', 'col')), may hold values from 0 to 127; in each aligned block of 128 rows (0 to 127, 128 to 255, ...) at most 2 rows name the same one
- block_cell: int32 [16384], P(('row', 'col')), may hold values from 0 to 255
- spec_weight: bfloat16 [64, 64, 16, 16, 128], P('col', 'row'), may hold values from -12 to 12
- skip_weight: bfloat16 [16, 16], replicated, may hold values from -1.5 to 1.5
- mlp_in: bfloat16 [64, 16], replicated, may hold values from -1.5 to 1.5
- mlp_bias: float32 [64], replicated, may hold values from -4 to 4
- mlp_out: bfloat16 [16, 64], replicated, may hold values from -0.75 to 0.75
Outputs:
- point_values: bfloat16 [16, 2097152], P(None, ('row', 'col'))
The draws below stay inside these ranges and needn't reach their ends.
Inputs may be any that keep to these rules, and one draw needn't show every extreme that they name: `block_owner`: in each aligned block of 128 rows (the point blocks of one device) no device number appears more than 2 times; devices are numbered r * 16 + s over row r and column s.
All inputs are finite; a program needn't handle non-finite values.
Results may differ from the reference program's by a relative error of at most 0.013.
Values may be sent and summed in bfloat16 or wider, within the bound.
No kernel may reach another device: no remote copies, remote signals or barrier semaphores. Data moves between devices by JAX's collectives and lax.ppermute only.
A program may use at most 128 MiB of HBM per device.

```python
import math
import jax
import jax.numpy as jnp
import numpy as np
from jax import lax

GRID = 256
CH = 16
MODES = 64
HID = 64
BE = 8
PB_PTS = 128
PB_DEV = 128
PBLOCKS = 16384
POINTS = 2097152
CAP = 2
XL = 32
YL = 16
BLK_DEV = 256
N_COL = 16
DEVICES = 128


def place_ends(array, stream_key, smallest, top_value):
    longest = array.shape.index(max(array.shape))
    spots = []
    for shift in (0, 1):
        where = [jax.random.randint(jax.random.fold_in(stream_key, axis), (), 0, length) for axis, length in enumerate(array.shape)]
        where[longest] = (where[longest] + shift) % array.shape[longest]
        spots.append(tuple(where))
    return array.at[spots[0]].set(smallest).at[spots[1]].set(top_value)


def levels(key, extent, split, low, largest):
    level, own = 1.0, jax.random.fold_in(key, 6)
    for position, parts in split:
        draws = jnp.exp(jax.random.uniform(jax.random.fold_in(own, position), (parts,), jnp.float32, low / len(split), largest / len(split)))
        level = level * jnp.repeat(draws, extent[position] // parts).reshape([-1 if axis == position else 1 for axis in range(len(extent))])
    return level


def deal_out(own_key, own, number, rows, count, top, reach, skew):
    ranking = jax.random.permutation(own_key, count)
    heavy_load, usual = shares(count, rows * top, reach, skew, True), shares(count, rows * top, reach, skew, False)
    places = jnp.arange(count)

    def named(lengths, turn):
        used = int((lengths > 0).sum())
        fixed = max(1, used // 4)
        shifted = fixed + (places - fixed + turn * (used - fixed)) % max(1, count - fixed)
        return jnp.zeros((count,), jnp.int32).at[ranking[jnp.where(places < fixed, places, shifted)]].set(jnp.asarray(lengths, jnp.int32))

    lengths = jnp.where(number % 4 == 0, named(heavy_load, number // 4), named(usual, number - number // 4 - 1))
    mixed = jax.random.permutation(jax.random.fold_in(own, 3), count)
    donor, taker = mixed[0:count // 2 * 2:2], mixed[1:count // 2 * 2:2]
    slack = jnp.minimum(lengths[donor] - 1, reach - lengths[taker]) // 2
    slack = jnp.where((donor == ranking[0]) | (taker == ranking[0]) | (lengths[taker] == 0), 0, jnp.maximum(slack, 0))
    shifted = jax.random.randint(jax.random.fold_in(own, 4), (count // 2,), 0, 1 << 20) % (slack + 1)
    lengths = lengths.at[donor].add(-shifted).at[taker].add(shifted)
    labels = jnp.searchsorted(jnp.cumsum(lengths), jnp.arange(rows * top), side="right").astype(jnp.int32)
    table = labels.reshape(top, rows).T
    table = table[jax.random.permutation(jax.random.fold_in(own, 1), rows)]
    turn = jax.random.randint(jax.random.fold_in(own, 2), (rows, 1), 0, top)
    return jnp.take_along_axis(table, (jnp.arange(top)[None, :] + turn) % top, axis=1)


def shares(amount, total, limit, slope, full):
    loads = [(1 << 20) // math.isqrt(rank ** slope) + 1 for rank in range(1, amount + 1)]
    largest = limit if full else min(limit, max(-(-total // amount), total * loads[0] // sum(loads)))
    least = 1 if total - largest >= amount - 1 else 0
    holding, spare = [largest] + [least] * (amount - 1), total - largest - least * (amount - 1)
    while spare > 0:
        movable = [i for i in range(1, amount) if holding[i] < largest] or [i for i in range(1, amount) if holding[i] < limit]
        whole, remaining = sum([loads[i] for i in movable]), spare
        for i in movable:
            more = min(limit - holding[i], max(1, remaining * loads[i] // whole), spare)
            holding[i] = holding[i] + more
            spare = spare - more
    return np.array(holding)


def bell_draw(stream_key, dims, deviation, most, split=(), held_as=jnp.bfloat16):
    result = jax.random.normal(stream_key, dims, jnp.float32) * deviation
    if len(split) > 0:
        result = levels(stream_key, dims, split, -0.22, 0.18) * result
    return jnp.clip(result, min=-most, max=most).astype(held_as)


def setup_inputs(seed: int = 0) -> dict:
    key_list = jax.random.split(jax.random.key(seed), 11)
    features = bell_draw(key_list[0], (CH, POINTS), 1.0, 6.0, ((1, 128),))
    point_weights = jnp.clip(0.049804688 + 0.9501953 * jax.random.uniform(key_list[1], (8, POINTS), jnp.float32) ** levels(key_list[1], (8, POINTS), ((1, 128),), -0.2, 0.2), 0.049804688, 1.0).astype(jnp.bfloat16)
    point_corner = place_ends(jax.random.randint(key_list[2], (POINTS,), 0, (BE - 1)**3), jax.random.fold_in(key_list[2], 1), 0, ((BE - 1)**3) - 1).astype(jnp.int32)
    block_owner_keys = jax.random.split(jax.random.fold_in(key_list[3], 1), PBLOCKS // PB_DEV)
    block_owner_turns = jax.random.permutation(jax.random.fold_in(key_list[3], 3), PBLOCKS // PB_DEV)
    block_owner = jax.vmap(lambda own, number: deal_out(jax.random.fold_in(key_list[3], 2), own, number, PB_DEV, DEVICES, 1, CAP, 2))(block_owner_keys, block_owner_turns).reshape((PBLOCKS, 1))
    block_cell = place_ends(jax.random.randint(key_list[4], (PBLOCKS,), 0, BLK_DEV), jax.random.fold_in(key_list[4], 1), 0, BLK_DEV - 1).astype(jnp.int32)
    spec_weight = bell_draw(key_list[5], (MODES, MODES, CH, CH, 2 * MODES), 2.0, 12.0, ((0, 16), (1, 8)))
    skip_weight = bell_draw(key_list[6], (CH, CH), CH ** -0.5, 1.5)
    mlp_in = bell_draw(key_list[7], (HID, CH), CH ** -0.5, 1.5)
    mlp_bias = bell_draw(key_list[8], (HID,), 1.0, 4.0, (), jnp.float32)
    mlp_out = bell_draw(key_list[9], (CH, HID), HID ** -0.5, 0.75)
    return {"features": features, "point_weights": point_weights, "point_corner": point_corner, "block_owner": block_owner, "block_cell": block_cell, "spec_weight": spec_weight, "skip_weight": skip_weight, "mlp_in": mlp_in, "mlp_bias": mlp_bias, "mlp_out": mlp_out}


def frequencies(count, length):
    index = jnp.arange(count, dtype=jnp.int32)
    return jnp.where(index < count // 2, index, length - count + index)

def angles(length, freq):
    places = jnp.arange(length, dtype=jnp.int32)
    turns = places[:, None] * freq[None, :] % length
    return 2.0 * math.pi / length * turns.astype(jnp.float32)

def forward_tables(length, count):
    factor = 1.0 / math.sqrt(length)
    theta = angles(length, jnp.arange(count, dtype=jnp.int32))
    real_basis_table = jnp.stack([jnp.cos(theta) * factor, -jnp.sin(theta) * factor], -1).reshape(length, 2 * count)
    theta = angles(length, frequencies(count, length))
    cosine = jnp.cos(theta) * factor
    sine = jnp.sin(theta) * factor
    from_real = jnp.stack([cosine, -sine], -1)
    from_imag = jnp.stack([sine, cosine], -1)
    paired = jnp.stack([from_real, from_imag], 0)
    planar = jnp.swapaxes(paired, 2, 3)
    return (real_basis_table.astype(jnp.bfloat16), paired.reshape(2, length, 2 * count).astype(jnp.bfloat16), planar.reshape(2, length, 2 * count).astype(jnp.bfloat16))

def inverse_tables(length, count):
    factor = 1.0 / math.sqrt(length)
    theta = angles(length, frequencies(count, length)).T
    cosine = jnp.cos(theta) * factor
    sine = jnp.sin(theta) * factor
    from_real = jnp.stack([cosine, sine], 1)
    from_imag = jnp.stack([-sine, cosine], 1)
    paired = jnp.stack([from_real, from_imag], 1)
    planar = jnp.swapaxes(paired, 0, 1)
    theta = angles(length, jnp.arange(count, dtype=jnp.int32)).T
    double = jnp.where(jnp.arange(count) == 0, 1.0, 2.0).astype(jnp.float32)[:, None]
    real_out = jnp.stack([double * jnp.cos(theta) * factor, -double * jnp.sin(theta) * factor], 1)
    return (real_out.reshape(2 * count, length).astype(jnp.bfloat16), paired.reshape(2 * count, 2, length).astype(jnp.bfloat16), planar.reshape(2 * count, 2, length).astype(jnp.bfloat16))

def corner_cell_indices(point_corner, edge_len):
    interior = edge_len - 1
    anchor = point_corner // (interior * interior) * edge_len * edge_len
    anchor = anchor + point_corner // interior % interior * edge_len + point_corner % interior
    corners = jnp.arange(8, dtype=jnp.int32)
    offsets = corners // 4 * edge_len * edge_len + corners // 2 % 2 * edge_len + corners % 2
    return (anchor[None, :] + offsets[:, None]).astype(jnp.int32)

def mix_modes(spectrum, weight):
    half = weight.shape[-1] // 2
    value_entries = spectrum.astype(jnp.float32)
    coeffs = weight.astype(jnp.float32)
    swapped = jnp.concatenate([value_entries[..., half:], value_entries[..., :half]], -1)
    real_part = jnp.concatenate([coeffs[..., :half], coeffs[..., :half]], -1)
    imag_part = jnp.concatenate([-coeffs[..., half:], coeffs[..., half:]], -1)
    total = value_entries[..., :, None, :] * real_part + swapped[..., :, None, :] * imag_part
    return lax.optimization_barrier(jnp.sum(total, axis=-3)).astype(jnp.bfloat16)

def reference(features, point_weights, point_corner, block_owner, block_cell, spec_weight, skip_weight, mlp_in, mlp_bias, mlp_out):
    block_cells = BE ** 3
    y_blocks = YL // BE
    z_blocks = GRID // BE
    owner = block_owner[:, 0]
    row_index = owner // N_COL
    col_index = owner % N_COL
    block_x = block_cell // (y_blocks * z_blocks)
    block_y = block_cell // z_blocks % y_blocks
    block_z = block_cell % z_blocks
    lanes = jnp.arange(block_cells, dtype=jnp.int32)
    cell_x = (row_index * XL + block_x * BE)[:, None] + (lanes // (BE * BE))[None, :]
    cell_y = (col_index * YL + block_y * BE)[:, None] + (lanes // BE % BE)[None, :]
    cell_z = (block_z * BE)[:, None] + (lanes % BE)[None, :]
    global_index = ((cell_x * GRID + cell_y) * GRID + cell_z).astype(jnp.int32)
    corner_cell = corner_cell_indices(point_corner, BE)
    point_block = (jnp.arange(POINTS, dtype=jnp.int32) // PB_PTS).astype(jnp.int32)
    segment_ids = (point_block[None, :] * block_cells + corner_cell).astype(jnp.int32)
    weights_f = point_weights.astype(jnp.float32)

    def scatter_channel(feature_row):
        value_entries = feature_row.astype(jnp.float32)[None, :] * weights_f
        partial_value = jax.ops.segment_sum(value_entries.reshape(-1), segment_ids.reshape(-1), num_segments=PBLOCKS * block_cells)
        partial_value = lax.optimization_barrier(partial_value.astype(jnp.bfloat16)).astype(jnp.float32)
        field = jnp.zeros((GRID ** 3,), jnp.float32).at[global_index.reshape(-1)].add(partial_value)
        return field.astype(jnp.bfloat16)
    grid = lax.map(scatter_channel, features)
    table_z, table_y, table_x = forward_tables(GRID, MODES)
    inv_z, inv_y, inv_x = inverse_tables(GRID, MODES)

    def forward(field):
        field = field.reshape(GRID * GRID, GRID)
        zspec = jnp.dot(field, table_z, preferred_element_type=jnp.float32).astype(jnp.bfloat16)
        moved = zspec.reshape(GRID, GRID, MODES, 2).transpose(0, 2, 3, 1).reshape(GRID * MODES, 2 * GRID)
        yspec = jnp.dot(moved, table_y.reshape(2 * GRID, 2 * MODES), preferred_element_type=jnp.float32).astype(jnp.bfloat16)
        moved = yspec.reshape(GRID, MODES, MODES, 2).transpose(1, 2, 3, 0).reshape(MODES * MODES, 2 * GRID)
        spec = jnp.dot(moved, table_x.reshape(2 * GRID, 2 * MODES), preferred_element_type=jnp.float32).astype(jnp.bfloat16)
        return spec.reshape(MODES, MODES, 2 * MODES)
    spectrum = lax.map(forward, grid)
    by_kz = spectrum.transpose(1, 2, 0, 3)

    def mix_slice(pair):
        return mix_modes(pair[0], pair[1])
    mixed = lax.map(mix_slice, (by_kz, spec_weight))
    mixed = mixed.transpose(2, 0, 1, 3)

    def inverse_xy(modes):
        xinv = jnp.dot(modes.reshape(MODES * MODES, 2 * MODES), inv_x.reshape(2 * MODES, 2 * GRID), preferred_element_type=jnp.float32).astype(jnp.bfloat16)
        moved = xinv.reshape(MODES, MODES, 2, GRID).transpose(0, 3, 1, 2).reshape(MODES * GRID, 2 * MODES)
        yinv = jnp.dot(moved, inv_y.reshape(2 * MODES, 2 * GRID), preferred_element_type=jnp.float32).astype(jnp.bfloat16)
        return yinv.reshape(MODES, GRID, 2, GRID)
    section = lax.map(inverse_xy, mixed)
    slab_len = 2
    slab_count = GRID // slab_len
    section_slabs = jnp.moveaxis(section.reshape(CH, MODES, slab_count, slab_len, 2, GRID), 2, 0)
    grid_slabs = jnp.moveaxis(grid.reshape(CH, slab_count, slab_len, GRID, GRID), 1, 0)
    inv_z_f = inv_z.astype(jnp.float32).reshape(MODES, 2, GRID)
    skip_f = skip_weight.astype(jnp.float32)
    first_f = mlp_in.astype(jnp.float32)
    second_f = mlp_out.astype(jnp.float32)
    high = lax.Precision.HIGHEST

    def layer_grid_plane(pair):
        modes, field = pair
        spectral = jnp.einsum('okxpy,kpz->oxyz', modes.astype(jnp.float32), inv_z_f, precision=high)
        pre = spectral + jnp.einsum('oi,ixyz->oxyz', skip_f, field.astype(jnp.float32), precision=high)
        pre = pre.astype(jnp.bfloat16).astype(jnp.float32)
        hidden = jnp.einsum('hi,ixyz->hxyz', first_f, pre, precision=high) + mlp_bias[:, None, None, None]
        hidden = jax.nn.gelu(hidden).astype(jnp.bfloat16).astype(jnp.float32)
        return jnp.einsum('oh,hxyz->oxyz', second_f, hidden, precision=high).astype(jnp.bfloat16)
    layer_grid = lax.map(layer_grid_plane, (section_slabs, grid_slabs))
    layer_grid = jnp.moveaxis(layer_grid, 0, 1).reshape(CH, GRID ** 3)
    point_index = global_index[point_block[None, :], corner_cell]

    def interpolate(field):
        picked = field[point_index].astype(jnp.float32)
        return lax.optimization_barrier(jnp.sum(picked * weights_f, axis=0)).astype(jnp.bfloat16)
    return lax.map(interpolate, layer_grid)
```

```python
import math
from functools import partial

import jax
import jax.numpy as jnp
import numpy as np
from jax import lax
from jax.experimental import pallas as pl
from jax.experimental.pallas import tpu as pltpu
from jax.sharding import PartitionSpec as P

GRID = 256
MODES = 64
BE = 8
NPTS = 128
NBLK = 128
NSLOT = 256
ROWS = 8
COLS = 16
CH = 16
HID = 64
F32 = jnp.float32
BF16 = jnp.bfloat16
NN = (((1,), (0,)), ((), ()))
NT = (((1,), (1,)), ((), ()))
TN = (((0,), (0,)), ((), ()))


def mm(a, b, dims=NN):
    return lax.dot_general(a, b, dims, preferred_element_type=F32)


def _freqs():
    j = np.arange(MODES)
    return np.where(j < MODES // 2, j, GRID - MODES + j)


def _trig(freq):
    turns = (np.arange(GRID)[:, None] * freq[None, :]) % GRID
    theta = (2.0 * math.pi / GRID) * turns
    f = 1.0 / math.sqrt(GRID)
    return np.cos(theta) * f, np.sin(theta) * f


def tables():
    cz, sz = _trig(np.arange(MODES))
    cf, sf = _trig(_freqs())
    tz = np.stack([cz, -sz], -1).reshape(GRID, 2 * MODES).T
    fwd = np.stack([np.stack([cf, -sf], -1), np.stack([sf, cf], -1)], 1)
    inv = np.stack(
        [np.stack([cf.T, sf.T], -1), np.stack([-sf.T, cf.T], -1)], 1
    )
    ty = fwd.reshape(COLS, 16, 2, ROWS, 8, 2).transpose(3, 5, 4, 0, 2, 1).reshape(128, 512)
    tx = fwd.reshape(ROWS, 4, 8, 2, MODES, 2).transpose(5, 4, 0, 1, 3, 2).reshape(128, 512)
    ix = inv.reshape(MODES, 2, ROWS, 4, 8, 2).transpose(2, 3, 5, 4, 1, 0).reshape(512, 128)
    iy = inv.reshape(ROWS, 8, 2, COLS, 16, 2).transpose(3, 5, 4, 0, 2, 1).reshape(512, 128)
    a = np.where(np.arange(MODES) == 0, 1.0, 2.0)[None, :]
    iz = np.stack([a * cz, -a * sz], -1).reshape(GRID, 2 * MODES)
    return [jnp.asarray(t.astype(np.float32)).astype(BF16) for t in (tz, ty, tx, ix, iy, iz)]


def div_const(v, d):
    return ((v.astype(F32) + 0.5) * (1.0 / d)).astype(jnp.int32)


def pack_kernel(own_ref, cell_ref, feat_ref, w_ref, corner_ref, send_ref, cnt_ref):
    zero = jnp.zeros((8, 32, NPTS), BF16)

    @pl.loop(0, NSLOT // 8)
    def _(i):
        send_ref[pl.ds(i * 8, 8)] = zero

    @pl.loop(0, NBLK)
    def _(i):
        cnt_ref[i] = 0

    row = lax.broadcasted_iota(jnp.int32, (8, NPTS), 0)

    @pl.loop(0, NBLK)
    def _(b):
        o = own_ref[b]
        r = cnt_ref[o]
        cnt_ref[o] = r + 1
        slot = o * 2 + jnp.minimum(r, 1)
        at = pl.multiple_of(b * NPTS, NPTS)
        v = jnp.broadcast_to(corner_ref[pl.ds(b, 1), :], (8, NPTS))
        vx = div_const(v, 49)
        rest = v - vx * 49
        vy = div_const(rest, 7)
        vz = rest - vy * 7
        head = jnp.where(
            row == 0, vx, jnp.where(row == 1, vy, jnp.where(row == 2, vz, cell_ref[b] + 1))
        )
        tail = jnp.concatenate([w_ref[:, pl.ds(at, NPTS)].astype(F32), head.astype(F32)], 0)
        send_ref[slot, 0:16, :] = feat_ref[:, pl.ds(at, NPTS)]
        send_ref[slot, 16:32, :] = tail.astype(BF16)


def pack(owner, cell, features, weights, corner):
    smem = pl.BlockSpec(memory_space=pltpu.SMEM)
    vmem = pl.BlockSpec(memory_space=pltpu.VMEM)
    return pl.pallas_call(
        pack_kernel,
        out_shape=jax.ShapeDtypeStruct((NSLOT, 32, NPTS), BF16),
        in_specs=[smem, smem, vmem, vmem, vmem],
        out_specs=vmem,
        scratch_shapes=[pltpu.SMEM((NBLK,), jnp.int32)],
        name="pack",
    )(owner, cell, features, weights, corner)


def yz_basis(tail):
    zi = lax.broadcasted_iota(jnp.int32, (8, NPTS), 0).astype(F32)
    bc = lambda k: jnp.broadcast_to(tail[k : k + 1, :], (8, NPTS))
    vy, vz = bc(9), bc(10)
    m0 = zi == vz
    m1 = zi == vz + 1.0
    zero = jnp.zeros((8, NPTS), F32)
    zc = [
        [
            jnp.where(m0, bc(4 * dx + 2 * dy), jnp.where(m1, bc(4 * dx + 2 * dy + 1), zero))
            for dy in range(2)
        ]
        for dx in range(2)
    ]
    my = [vy == float(y) for y in range(7)]
    halves = []
    for dx in range(2):
        rows = []
        for y in range(8):
            val = zero
            if y > 0:
                val = jnp.where(my[y - 1], zc[dx][1], val)
            if y < 7:
                val = jnp.where(my[y], zc[dx][0], val)
            rows.append(val)
        halves.append(jnp.concatenate(rows, 0).astype(BF16))
    return jnp.concatenate(halves, 1)


def scatter_kernel(ids_ref, recv_ref, tz_ref, field_ref, out_ref, g_ref, z_ref, *, unroll):
    zero = jnp.zeros((4, 64, 128), F32)

    @pl.loop(0, 64)
    def _(i):
        g_ref[pl.ds(i * 4, 4)] = zero

    @pl.loop(0, NSLOT // unroll)
    def _(i):
        for u in range(unroll):
            s = i * unroll + u
            tail = recv_ref[s, 16:32, :].astype(F32)
            basis = yz_basis(tail)
            feat = recv_ref[s, 0:16, :].astype(F32)
            vx = jnp.broadcast_to(tail[8:9, :], (16, NPTS))
            zf = jnp.zeros((16, NPTS), BF16)
            part = [jnp.where(vx == float(x), feat, 0.0).astype(BF16) for x in range(7)]
            lhs = jnp.concatenate(
                [jnp.concatenate(part + [zf], 0), jnp.concatenate([zf] + part, 0)], 1
            )
            res = mm(basis, lhs, NT)
            b = jnp.maximum(ids_ref[s] - 1, 0)
            g_ref[b] = g_ref[b] + res

    tz = tz_ref[...]

    @pl.loop(0, 8)
    def _(q):
        bx = q // 2
        by = q % 2
        for yl in range(8):
            m = g_ref[pl.ds(q * 32, 32), yl * 8 : yl * 8 + 8, :].reshape(GRID, 128).astype(BF16)
            field_ref[q * 8 + yl] = m
            z_ref[bx, pl.ds(by * 8 + yl, 128, stride=16), :] = mm(tz, m)

    @pl.loop(0, 16)
    def _(s):
        for k in range(8):
            for bx in range(4):
                at = pl.multiple_of(s * 128 + k * 16, 16)
                out_ref[s, k, bx] = z_ref[bx, pl.ds(at, 16), :].astype(BF16)


def scatter(ids, recv, tz):
    smem = pl.BlockSpec(memory_space=pltpu.SMEM)
    vmem = pl.BlockSpec(memory_space=pltpu.VMEM)
    return pl.pallas_call(
        partial(scatter_kernel, unroll=4),
        out_shape=(
            jax.ShapeDtypeStruct((64, GRID, 128), BF16),
            jax.ShapeDtypeStruct((16, 8, 4, 16, 128), BF16),
        ),
        in_specs=[smem, vmem, vmem],
        out_specs=(vmem, vmem),
        scratch_shapes=[pltpu.VMEM((256, 64, 128), F32), pltpu.VMEM((4, 2048, 128), F32)],
        name="scatter_z",
    )(ids, recv, tz)


def y_kernel(in_ref, t_ref, out_ref):
    t = t_ref[...]
    for kz in range(4):
        for h in range(2):
            rhs = jnp.concatenate(
                [in_ref[:, 2 * kz : 2 * kz + 2, 2 * h + e].reshape(512, 128) for e in range(2)], 1
            )
            res = mm(t, rhs).astype(BF16)
            for r in range(8):
                for e in range(2):
                    out_ref[r, kz, 2 * h + e] = res[r * 16 : r * 16 + 16, e * 128 : e * 128 + 128]


def y_forward(zs, ty):
    return pl.pallas_call(
        y_kernel,
        out_shape=jax.ShapeDtypeStruct((8, 4, 4, 16, 128), BF16),
        name="y_forward",
    )(zs, ty)


def block_transpose(x):
    si = lax.broadcasted_iota(jnp.int32, x.shape, 1)
    gi = lax.broadcasted_iota(jnp.int32, x.shape, 2) // 16
    for k in range(3):
        d = 1 << k
        mi = (si // d) % 2
        mg = (gi // d) % 2
        up = pltpu.roll(pltpu.roll(x, 8 - d, 1), 16 * d, 2)
        if k == 2:
            x = jnp.where(mi == mg, x, up)
        else:
            down = pltpu.roll(pltpu.roll(x, d, 1), 128 - 16 * d, 2)
            x = jnp.where(mi == mg, x, jnp.where(mi < mg, up, down))
    return x


def x_kernel(in_ref, w_ref, tx_ref, ix_ref, out_ref):
    data = in_ref[...].astype(F32).reshape(64, 8, 128)
    data = block_transpose(data).reshape(512, 128).astype(BF16)
    spec = mm(tx_ref[...], data).T.astype(BF16).astype(F32)
    swapped = pltpu.roll(spec, 64, 1)
    lane = lax.broadcasted_iota(jnp.int32, (16, 128), 1)
    parts = []
    for ky in range(8):
        a1 = jnp.zeros((16, 128), F32)
        a2 = jnp.zeros((16, 128), F32)
        for c in range(CH):
            w = w_ref[0, ky, c].astype(F32)
            at = ky * 16 + c
            a1 = a1 + spec[at : at + 1, :] * w
            a2 = a2 + swapped[at : at + 1, :] * w
        parts.append(
            jnp.where(lane < 64, a1 - pltpu.roll(a1, 64, 1), a2 + pltpu.roll(a2, 64, 1))
        )
    mixed = jnp.concatenate(parts, 0).astype(BF16)
    xi = mm(ix_ref[...], mixed, NT)
    xi = block_transpose(xi.reshape(64, 8, 128))
    out_ref[...] = xi.reshape(8, 1, 4, 16, 128).astype(BF16)


def x_mix(ys, weight, tx, ix):
    whole = lambda k: (0, 0)
    return pl.pallas_call(
        x_kernel,
        grid=(4,),
        out_shape=jax.ShapeDtypeStruct((8, 4, 4, 16, 128), BF16),
        in_specs=[
            pl.BlockSpec((8, 1, 4, 16, 128), lambda k: (0, k, 0, 0, 0)),
            pl.BlockSpec((1, 8, 16, 16, 128), lambda k: (k, 0, 0, 0, 0)),
            pl.BlockSpec((128, 512), whole),
            pl.BlockSpec((512, 128), whole),
        ],
        out_specs=pl.BlockSpec((8, 1, 4, 16, 128), lambda k: (0, k, 0, 0, 0)),
        name="x_mix",
    )(ys, weight, tx, ix)


def yi_kernel(in_ref, t_ref, out_ref):
    t = t_ref[...]
    for kz in range(4):
        for h in range(2):
            rhs = jnp.concatenate(
                [in_ref[:, kz, 2 * h + e].reshape(128, 128) for e in range(2)], 1
            )
            res = mm(t, rhs).astype(BF16)
            for s in range(16):
                for ri in range(2):
                    at = s * 32 + ri * 16
                    for e in range(2):
                        out_ref[s, 2 * kz + ri, 2 * h + e] = res[
                            at : at + 16, e * 128 : e * 128 + 128
                        ]


def y_inverse(xs, iy):
    return pl.pallas_call(
        yi_kernel,
        out_shape=jax.ShapeDtypeStruct((16, 8, 4, 16, 128), BF16),
        name="y_inverse",
    )(xs, iy)


def final_kernel(
    ids_ref, yi_ref, field_ref, tail_ref, iz_ref, sk_ref, w1_ref, b1_ref, w2_ref,
    out_ref, y_ref, l_ref, *, unroll
):
    @pl.loop(0, 16)
    def _(s):
        for k in range(8):
            for bx in range(4):
                at = pl.multiple_of(s * 128 + k * 16, 16)
                y_ref[bx, pl.ds(at, 16), :] = yi_ref[s, k, bx].astype(F32)

    iz = iz_ref[...]
    sk = sk_ref[...]
    w1 = w1_ref[...]
    w2 = w2_ref[...]
    b1 = b1_ref[...]

    @pl.loop(0, 64)
    def _(i):
        bx = i // 16
        y = i % 16
        rhs = y_ref[bx, pl.ds(y, 128, stride=16), :].astype(BF16)
        pre = (mm(iz, rhs) + mm(field_ref[i], sk)).astype(BF16)
        h = jax.nn.gelu(mm(pre, w1) + b1).astype(BF16)
        l_ref[i] = mm(h, w2).astype(BF16).astype(F32)

    @pl.loop(0, NSLOT // unroll)
    def _(i):
        for u in range(unroll):
            s = i * unroll + u
            tail = tail_ref[s].astype(F32)
            basis = yz_basis(tail)
            b = jnp.maximum(ids_ref[s] - 1, 0)
            q = b // 32
            at = pl.multiple_of((b % 32) * 8, 8)
            cells = l_ref[pl.ds(q * 8, 8), pl.ds(at, 8), :].reshape(64, 128).astype(BF16)
            res = mm(cells, basis, TN)
            vx = jnp.broadcast_to(tail[8:9, :], (16, NPTS))
            val = jnp.zeros((16, NPTS), F32)
            for x in range(7):
                got = res[x * 16 : x * 16 + 16, 0:128] + res[x * 16 + 16 : x * 16 + 32, 128:256]
                val = jnp.where(vx == float(x), got, val)
            out_ref[s] = val.astype(BF16)


def final(ids, yi, field, recv, iz, sk, w1, b1, w2):
    smem = pl.BlockSpec(memory_space=pltpu.SMEM)
    vmem = pl.BlockSpec(memory_space=pltpu.VMEM)
    return pl.pallas_call(
        partial(final_kernel, unroll=4),
        grid=(1,),
        out_shape=jax.ShapeDtypeStruct((NSLOT, 16, NPTS), BF16),
        in_specs=[
            smem,
            vmem,
            vmem,
            pl.BlockSpec((NSLOT, 16, NPTS), lambda i: (0, 1, 0)),
            vmem,
            vmem,
            vmem,
            vmem,
            vmem,
        ],
        out_specs=vmem,
        scratch_shapes=[pltpu.VMEM((4, 2048, 128), F32), pltpu.VMEM((64, GRID, 128), F32)],
        name="mlp_gather",
    )(ids, yi, field, recv, iz, sk, w1, b1, w2)


def unpack_kernel(own_ref, in_ref, out_ref, cnt_ref):
    @pl.loop(0, NBLK)
    def _(i):
        cnt_ref[i] = 0

    @pl.loop(0, NBLK)
    def _(b):
        o = own_ref[b]
        r = cnt_ref[o]
        cnt_ref[o] = r + 1
        slot = o * 2 + jnp.minimum(r, 1)
        at = pl.multiple_of(b * NPTS, NPTS)
        out_ref[:, pl.ds(at, NPTS)] = in_ref[slot]


def unpack(owner, vals):
    smem = pl.BlockSpec(memory_space=pltpu.SMEM)
    vmem = pl.BlockSpec(memory_space=pltpu.VMEM)
    return pl.pallas_call(
        unpack_kernel,
        out_shape=jax.ShapeDtypeStruct((CH, NBLK * NPTS), BF16),
        in_specs=[smem, vmem],
        out_specs=vmem,
        scratch_shapes=[pltpu.SMEM((NBLK,), jnp.int32)],
        name="unpack",
    )(owner, vals)


def a2a(x, axes):
    return lax.all_to_all(x, axes, split_axis=0, concat_axis=0, tiled=True)


def body(
    features,
    point_weights,
    point_corner,
    block_owner,
    block_cell,
    spec_weight,
    skip_weight,
    mlp_in,
    mlp_bias,
    mlp_out,
):
    tz, ty, tx, ix, iy, iz = tables()
    eye = jnp.eye(8, dtype=BF16)
    sk = jnp.kron(eye, skip_weight.T)
    w1 = jnp.kron(eye, mlp_in.T)
    w2 = jnp.kron(eye, mlp_out.T)
    b1 = jnp.tile(mlp_bias, 8)[None, :]
    owner = block_owner.reshape(NBLK)
    send = pack(owner, block_cell, features, point_weights, point_corner.reshape(NBLK, NPTS))
    recv = a2a(send, ("row", "col"))
    ids = recv[:, 27, 0].astype(jnp.int32)
    field, zs = scatter(ids, recv, tz)
    zs = a2a(zs, "col")
    ys = y_forward(zs, ty)
    ys = a2a(ys, "row")
    xs = x_mix(ys, spec_weight, tx, ix)
    xs = a2a(xs, "row")
    yi = y_inverse(xs, iy)
    yi = a2a(yi, "col")
    vals = final(ids, yi, field, recv, iz, sk, w1, b1, w2)
    vals = a2a(vals, ("row", "col"))
    return unpack(owner, vals)


def solution(mesh):
    return jax.shard_map(
        body,
        mesh=mesh,
        in_specs=(
            P(None, ("row", "col")),
            P(None, ("row", "col")),
            P(("row", "col")),
            P(("row", "col"), None),
            P(("row", "col")),
            P("col", "row", None, None, None),
            P(),
            P(),
            P(),
            P(),
        ),
        out_specs=P(None, ("row", "col")),
        check_vma=False,
    )
```

```python
import math
from functools import partial

import jax
import jax.numpy as jnp
import numpy as np
from jax import lax
from jax.experimental import pallas as pl
from jax.experimental.pallas import tpu as pltpu
from jax.sharding import PartitionSpec as P

GRID = 256
MODES = 64
BE = 8
NPTS = 128
NBLK = 128
NSLOT = 256
ROWS = 8
COLS = 16
CH = 16
HID = 64
F32 = jnp.float32
BF16 = jnp.bfloat16
NN = (((1,), (0,)), ((), ()))
NT = (((1,), (1,)), ((), ()))
TN = (((0,), (0,)), ((), ()))


def mm(a, b, dims=NN):
    return lax.dot_general(a, b, dims, preferred_element_type=F32)


def _freqs():
    j = np.arange(MODES)
    return np.where(j < MODES // 2, j, GRID - MODES + j)


def _trig(freq):
    turns = (np.arange(GRID)[:, None] * freq[None, :]) % GRID
    theta = (2.0 * math.pi / GRID) * turns
    f = 1.0 / math.sqrt(GRID)
    return np.cos(theta) * f, np.sin(theta) * f


def tables():
    cz, sz = _trig(np.arange(MODES))
    cf, sf = _trig(_freqs())
    tz = np.stack([cz, -sz], -1).reshape(GRID, 2 * MODES).T
    fwd = np.stack([np.stack([cf, -sf], -1), np.stack([sf, cf], -1)], 1)
    inv = np.stack(
        [np.stack([cf.T, sf.T], -1), np.stack([-sf.T, cf.T], -1)], 1
    )
    ty = fwd.reshape(COLS, 16, 2, ROWS, 8, 2).transpose(3, 5, 4, 0, 2, 1).reshape(128, 512)
    tx = fwd.reshape(ROWS, 4, 8, 2, MODES, 2).transpose(5, 4, 0, 1, 3, 2).reshape(128, 512)
    ix = inv.reshape(MODES, 2, ROWS, 4, 8, 2).transpose(2, 3, 5, 4, 1, 0).reshape(512, 128)
    iy = inv.reshape(ROWS, 8, 2, COLS, 16, 2).transpose(3, 5, 4, 0, 2, 1).reshape(512, 128)
    a = np.where(np.arange(MODES) == 0, 1.0, 2.0)[None, :]
    iz = np.stack([a * cz, -a * sz], -1).reshape(GRID, 2 * MODES)
    return [jnp.asarray(t.astype(np.float32)).astype(BF16) for t in (tz, ty, tx, ix, iy, iz)]


def div_const(v, d):
    return ((v.astype(F32) + 0.5) * (1.0 / d)).astype(jnp.int32)


def pack_kernel(own_ref, cell_ref, feat_ref, w_ref, corner_ref, send_ref, cnt_ref):
    zero = jnp.zeros((8, 32, NPTS), BF16)

    @pl.loop(0, NSLOT // 8)
    def _(i):
        send_ref[pl.ds(i * 8, 8)] = zero

    @pl.loop(0, NBLK, unroll=16)
    def _(i):
        cnt_ref[i] = 0

    row = lax.broadcasted_iota(jnp.int32, (8, NPTS), 0)

    @pl.loop(0, NBLK, unroll=8)
    def _(b):
        o = own_ref[b]
        r = cnt_ref[o]
        cnt_ref[o] = r + 1
        slot = o * 2 + jnp.minimum(r, 1)
        at = pl.multiple_of(b * NPTS, NPTS)
        v = jnp.broadcast_to(corner_ref[pl.ds(b, 1), :], (8, NPTS))
        vx = div_const(v, 49)
        rest = v - vx * 49
        vy = div_const(rest, 7)
        vz = rest - vy * 7
        head = jnp.where(
            row == 0, vx, jnp.where(row == 1, vy, jnp.where(row == 2, vz, cell_ref[b] + 1))
        )
        tail = jnp.concatenate([w_ref[:, pl.ds(at, NPTS)].astype(F32), head.astype(F32)], 0)
        send_ref[slot, 0:16, :] = feat_ref[:, pl.ds(at, NPTS)]
        send_ref[slot, 16:32, :] = tail.astype(BF16)


def pack(owner, cell, features, weights, corner):
    smem = pl.BlockSpec(memory_space=pltpu.SMEM)
    vmem = pl.BlockSpec(memory_space=pltpu.VMEM)
    return pl.pallas_call(
        pack_kernel,
        out_shape=jax.ShapeDtypeStruct((NSLOT, 32, NPTS), BF16),
        in_specs=[smem, smem, vmem, vmem, vmem],
        out_specs=vmem,
        scratch_shapes=[pltpu.SMEM((NBLK,), jnp.int32)],
        name="pack",
    )(owner, cell, features, weights, corner)


def yz_basis(tail):
    zi = lax.broadcasted_iota(jnp.int32, (8, NPTS), 0).astype(F32)
    bc = lambda k: jnp.broadcast_to(tail[k : k + 1, :], (8, NPTS))
    vy, vz = bc(9), bc(10)
    m0 = zi == vz
    m1 = zi == vz + 1.0
    zero = jnp.zeros((8, NPTS), F32)
    zc = [
        [
            jnp.where(m0, bc(4 * dx + 2 * dy), jnp.where(m1, bc(4 * dx + 2 * dy + 1), zero))
            for dy in range(2)
        ]
        for dx in range(2)
    ]
    my = [vy == float(y) for y in range(7)]
    halves = []
    for dx in range(2):
        rows = []
        for y in range(8):
            val = zero
            if y > 0:
                val = jnp.where(my[y - 1], zc[dx][1], val)
            if y < 7:
                val = jnp.where(my[y], zc[dx][0], val)
            rows.append(val)
        halves.append(jnp.concatenate(rows, 0).astype(BF16))
    return jnp.concatenate(halves, 1)


def scatter_kernel(
    recv_hbm, tz_ref, field_hbm, out_hbm, ids_ref,
    recv_ref, g_ref, z_ref, field_ref, out_ref, in_sem, field_sem, out_sem, *, unroll
):
    part = NSLOT // 4

    def fetch(k):
        at = pl.ds(k * part, part)
        return pltpu.make_async_copy(recv_hbm.at[at], recv_ref.at[at], in_sem.at[k])

    for k in range(4):
        fetch(k).start()
    zero = jnp.zeros((4, 64, 128), F32)

    @pl.loop(0, 64)
    def _(i):
        g_ref[pl.ds(i * 4, 4)] = zero

    @pl.loop(0, 4)
    def _(k):
        fetch(k).wait()

        @pl.loop(0, part // unroll)
        def _(i):
            for u in range(unroll):
                s = k * part + i * unroll + u
                tail = recv_ref[s, 16:32, :].astype(F32)
                basis = yz_basis(tail)
                feat = recv_ref[s, 0:16, :].astype(F32)
                vx = jnp.broadcast_to(tail[8:9, :], (16, NPTS))
                zf = jnp.zeros((16, NPTS), BF16)
                sel = [jnp.where(vx == float(x), feat, 0.0).astype(BF16) for x in range(7)]
                lhs = jnp.concatenate(
                    [jnp.concatenate(sel + [zf], 0), jnp.concatenate([zf] + sel, 0)], 1
                )
                res = mm(basis, lhs, NT)
                b = jnp.clip(tail[11, 0].astype(jnp.int32) - 1, 0, 255)
                ids_ref[s] = b
                g_ref[b] = g_ref[b] + res

    tz = tz_ref[...]

    def put_field(q):
        at = pl.ds(q * 8, 8)
        return pltpu.make_async_copy(field_ref.at[at], field_hbm.at[at], field_sem.at[q])

    def put_out(s):
        return pltpu.make_async_copy(out_ref.at[s], out_hbm.at[s], out_sem.at[s])

    @pl.loop(0, 8)
    def _(q):
        bx = q // 2
        by = q % 2
        for h in range(4):
            ms = []
            for yl in (2 * h, 2 * h + 1):
                m = g_ref[pl.ds(q * 32, 32), yl * 8 : yl * 8 + 8, :].reshape(GRID, 128)
                m = m.astype(BF16)
                field_ref[q * 8 + yl] = m
                ms.append(m)
            res = mm(tz, jnp.concatenate(ms, 1))
            for e in range(2):
                y = by * 8 + 2 * h + e
                z_ref[bx, pl.ds(y, 128, stride=16), :] = res[:, e * 128 : e * 128 + 128]
        put_field(q).start()

    @pl.loop(0, 16)
    def _(s):
        for k in range(8):
            for bx in range(4):
                at = pl.multiple_of(s * 128 + k * 16, 16)
                out_ref[s, k, bx] = z_ref[bx, pl.ds(at, 16), :].astype(BF16)
        put_out(s).start()

    @pl.loop(0, 8)
    def _(q):
        put_field(q).wait()

    @pl.loop(0, 16)
    def _(s):
        put_out(s).wait()


def scatter(recv, tz):
    smem = pl.BlockSpec(memory_space=pltpu.SMEM)
    vmem = pl.BlockSpec(memory_space=pltpu.VMEM)
    hbm = pl.BlockSpec(memory_space=pl.ANY)
    return pl.pallas_call(
        partial(scatter_kernel, unroll=16),
        out_shape=(
            jax.ShapeDtypeStruct((64, GRID, 128), BF16),
            jax.ShapeDtypeStruct((16, 8, 4, 16, 128), BF16),
            jax.ShapeDtypeStruct((NSLOT,), jnp.int32),
        ),
        in_specs=[hbm, vmem],
        out_specs=(hbm, hbm, smem),
        scratch_shapes=[
            pltpu.VMEM((NSLOT, 32, NPTS), BF16),
            pltpu.VMEM((256, 64, 128), F32),
            pltpu.VMEM((4, 2048, 128), F32),
            pltpu.VMEM((64, GRID, 128), BF16),
            pltpu.VMEM((16, 8, 4, 16, 128), BF16),
            pltpu.SemaphoreType.DMA((4,)),
            pltpu.SemaphoreType.DMA((8,)),
            pltpu.SemaphoreType.DMA((16,)),
        ],
        name="scatter_z",
    )(recv, tz)


def y_kernel(in_ref, t_ref, out_ref):
    t = t_ref[...]
    for kz in range(4):
        for h in range(2):
            rhs = jnp.concatenate(
                [in_ref[:, 2 * kz : 2 * kz + 2, 2 * h + e].reshape(512, 128) for e in range(2)], 1
            )
            res = mm(t, rhs).astype(BF16)
            for r in range(8):
                for e in range(2):
                    out_ref[r, kz, 2 * h + e] = res[r * 16 : r * 16 + 16, e * 128 : e * 128 + 128]


def y_forward(zs, ty):
    return pl.pallas_call(
        y_kernel,
        out_shape=jax.ShapeDtypeStruct((8, 4, 4, 16, 128), BF16),
        name="y_forward",
    )(zs, ty)


def block_transpose(x):
    si = lax.broadcasted_iota(jnp.int32, x.shape, 1)
    gi = lax.broadcasted_iota(jnp.int32, x.shape, 2) // 16
    for k in range(3):
        d = 1 << k
        mi = (si // d) % 2
        mg = (gi // d) % 2
        up = pltpu.roll(pltpu.roll(x, 8 - d, 1), 16 * d, 2)
        if k == 2:
            x = jnp.where(mi == mg, x, up)
        else:
            down = pltpu.roll(pltpu.roll(x, d, 1), 128 - 16 * d, 2)
            x = jnp.where(mi == mg, x, jnp.where(mi < mg, up, down))
    return x


def x_kernel(in_ref, w_ref, tx_ref, ix_ref, out_ref):
    data = in_ref[...].astype(F32).reshape(64, 8, 128)
    data = block_transpose(data).reshape(512, 128).astype(BF16)
    spec = mm(tx_ref[...], data).T.astype(BF16).astype(F32)
    swapped = pltpu.roll(spec, 64, 1)
    lane = lax.broadcasted_iota(jnp.int32, (16, 128), 1)
    parts = []
    for ky in range(8):
        a1 = jnp.zeros((16, 128), F32)
        a2 = jnp.zeros((16, 128), F32)
        for c in range(CH):
            w = w_ref[0, ky, c].astype(F32)
            at = ky * 16 + c
            a1 = a1 + spec[at : at + 1, :] * w
            a2 = a2 + swapped[at : at + 1, :] * w
        parts.append(
            jnp.where(lane < 64, a1 - pltpu.roll(a1, 64, 1), a2 + pltpu.roll(a2, 64, 1))
        )
    mixed = jnp.concatenate(parts, 0).astype(BF16)
    xi = mm(ix_ref[...], mixed, NT)
    xi = block_transpose(xi.reshape(64, 8, 128))
    out_ref[...] = xi.reshape(8, 1, 4, 16, 128).astype(BF16)


def x_mix(ys, weight, tx, ix):
    whole = lambda k: (0, 0)
    return pl.pallas_call(
        x_kernel,
        grid=(4,),
        out_shape=jax.ShapeDtypeStruct((8, 4, 4, 16, 128), BF16),
        in_specs=[
            pl.BlockSpec((8, 1, 4, 16, 128), lambda k: (0, k, 0, 0, 0)),
            pl.BlockSpec((1, 8, 16, 16, 128), lambda k: (k, 0, 0, 0, 0)),
            pl.BlockSpec((128, 512), whole),
            pl.BlockSpec((512, 128), whole),
        ],
        out_specs=pl.BlockSpec((8, 1, 4, 16, 128), lambda k: (0, k, 0, 0, 0)),
        name="x_mix",
    )(ys, weight, tx, ix)


def yi_kernel(in_ref, t_ref, out_ref):
    t = t_ref[...]
    for kz in range(4):
        for h in range(2):
            rhs = jnp.concatenate(
                [in_ref[:, kz, 2 * h + e].reshape(128, 128) for e in range(2)], 1
            )
            res = mm(t, rhs).astype(BF16)
            for s in range(16):
                for ri in range(2):
                    at = s * 32 + ri * 16
                    for e in range(2):
                        out_ref[s, 2 * kz + ri, 2 * h + e] = res[
                            at : at + 16, e * 128 : e * 128 + 128
                        ]


def y_inverse(xs, iy):
    return pl.pallas_call(
        yi_kernel,
        out_shape=jax.ShapeDtypeStruct((16, 8, 4, 16, 128), BF16),
        name="y_inverse",
    )(xs, iy)


def gelu(x):
    x = x.astype(BF16)
    c = math.sqrt(2.0 / math.pi)
    t = jnp.tanh(x * (jnp.asarray(c, BF16) + jnp.asarray(c * 0.044715, BF16) * (x * x)))
    h = x * jnp.asarray(0.5, BF16)
    return h + h * t


def final_kernel(
    ids_ref, yi_hbm, field_hbm, recv_hbm, iz_ref, w1_ref, b1_ref, w2_ref, out_hbm,
    yi_ref, field_ref, tail_ref, out_ref, y_ref, x_ref, l_ref,
    yi_sem, field_sem, tail_sem, out_sem, *, ny, unroll
):
    def get_yi(s):
        return pltpu.make_async_copy(yi_hbm.at[s], yi_ref.at[s], yi_sem.at[s])

    def get_field(i):
        at = pl.ds(i * ny, ny)
        return pltpu.make_async_copy(field_hbm.at[at], field_ref.at[at], field_sem.at[i])

    def put_out(i):
        at = pl.ds(i * unroll, unroll)
        return pltpu.make_async_copy(out_ref.at[at], out_hbm.at[at], out_sem.at[i])

    get_tail = pltpu.make_async_copy(recv_hbm.at[:, 16:32], tail_ref, tail_sem)

    @pl.loop(0, 16)
    def _(s):
        get_yi(s).start()

    @pl.loop(0, 64 // ny)
    def _(i):
        get_field(i).start()

    get_tail.start()

    @pl.loop(0, 16)
    def _(s):
        get_yi(s).wait()
        for k in range(8):
            for bx in range(4):
                at = pl.multiple_of(s * 128 + k * 16, 16)
                y_ref[bx, pl.ds(at, 16), :] = yi_ref[s, k, bx].astype(F32)

    @pl.loop(0, 64 // ny)
    def _(i):
        base = i * ny
        bx = base // 16
        get_field(i).wait()
        for p in range(ny // 2):
            y = (base + 2 * p) % 16
            rhs = jnp.concatenate(
                [y_ref[bx, pl.ds(y + e, 128, stride=16), :] for e in range(2)], 1
            ).astype(BF16)
            res = mm(iz_ref[...], rhs).astype(BF16)
            for e in range(2):
                at = (2 * p + e) * GRID
                x_ref[at : at + GRID, 0:128] = res[:, e * 128 : e * 128 + 128]
                x_ref[at : at + GRID, 128:256] = field_ref[base + 2 * p + e]
        h = gelu(mm(x_ref[...], w1_ref[...]) + b1_ref[...])
        o = mm(h, w2_ref[...]).astype(BF16).astype(F32)
        l_ref[pl.ds(base, ny)] = o.reshape(ny, GRID, 128)

    get_tail.wait()

    @pl.loop(0, NSLOT // unroll)
    def _(i):
        for u in range(unroll):
            s = i * unroll + u
            tail = tail_ref[s].astype(F32)
            basis = yz_basis(tail)
            b = ids_ref[s]
            q = b // 32
            at = pl.multiple_of((b % 32) * 8, 8)
            cells = l_ref[pl.ds(q * 8, 8), pl.ds(at, 8), :].reshape(64, 128).astype(BF16)
            res = mm(cells, basis, TN)
            vx = jnp.broadcast_to(tail[8:9, :], (16, NPTS))
            val = jnp.zeros((16, NPTS), F32)
            for x in range(7):
                got = res[x * 16 : x * 16 + 16, 0:128] + res[x * 16 + 16 : x * 16 + 32, 128:256]
                val = jnp.where(vx == float(x), got, val)
            out_ref[s] = val.astype(BF16)
        put_out(i).start()

    @pl.loop(0, NSLOT // unroll)
    def _(i):
        put_out(i).wait()


def final(ids, yi, field, recv, iz, w1, b1, w2):
    smem = pl.BlockSpec(memory_space=pltpu.SMEM)
    vmem = pl.BlockSpec(memory_space=pltpu.VMEM)
    hbm = pl.BlockSpec(memory_space=pl.ANY)
    ny, unroll = 8, 32
    return pl.pallas_call(
        partial(final_kernel, ny=ny, unroll=unroll),
        out_shape=jax.ShapeDtypeStruct((NSLOT, 16, NPTS), BF16),
        in_specs=[smem, hbm, hbm, hbm, vmem, vmem, vmem, vmem],
        out_specs=hbm,
        scratch_shapes=[
            pltpu.VMEM((16, 8, 4, 16, 128), BF16),
            pltpu.VMEM((64, GRID, 128), BF16),
            pltpu.VMEM((NSLOT, 16, NPTS), BF16),
            pltpu.VMEM((NSLOT, 16, NPTS), BF16),
            pltpu.VMEM((4, 2048, 128), F32),
            pltpu.VMEM((ny * GRID, 256), BF16),
            pltpu.VMEM((64, GRID, 128), F32),
            pltpu.SemaphoreType.DMA((16,)),
            pltpu.SemaphoreType.DMA((64 // ny,)),
            pltpu.SemaphoreType.DMA,
            pltpu.SemaphoreType.DMA((NSLOT // unroll,)),
        ],
        name="mlp_gather",
    )(ids, yi, field, recv, iz, w1, b1, w2)


def unpack_kernel(own_ref, in_ref, out_ref, cnt_ref):
    @pl.loop(0, NBLK, unroll=16)
    def _(i):
        cnt_ref[i] = 0

    @pl.loop(0, NBLK, unroll=8)
    def _(b):
        o = own_ref[b]
        r = cnt_ref[o]
        cnt_ref[o] = r + 1
        slot = o * 2 + jnp.minimum(r, 1)
        at = pl.multiple_of(b * NPTS, NPTS)
        out_ref[:, pl.ds(at, NPTS)] = in_ref[slot]


def unpack(owner, vals):
    smem = pl.BlockSpec(memory_space=pltpu.SMEM)
    vmem = pl.BlockSpec(memory_space=pltpu.VMEM)
    return pl.pallas_call(
        unpack_kernel,
        out_shape=jax.ShapeDtypeStruct((CH, NBLK * NPTS), BF16),
        in_specs=[smem, vmem],
        out_specs=vmem,
        scratch_shapes=[pltpu.SMEM((NBLK,), jnp.int32)],
        name="unpack",
    )(owner, vals)


def a2a(x, axes):
    return lax.all_to_all(x, axes, split_axis=0, concat_axis=0, tiled=True)


def body(
    features,
    point_weights,
    point_corner,
    block_owner,
    block_cell,
    spec_weight,
    skip_weight,
    mlp_in,
    mlp_bias,
    mlp_out,
):
    tz, ty, tx, ix, iy, iz = tables()
    eye = jnp.eye(8, dtype=BF16)
    both = jnp.dot(mlp_in, skip_weight, preferred_element_type=F32).astype(BF16)
    w1 = jnp.concatenate([jnp.kron(eye, mlp_in.T), jnp.kron(eye, both.T)], 0)
    w2 = jnp.kron(eye, mlp_out.T)
    b1 = jnp.tile(mlp_bias, 8)[None, :]
    owner = block_owner.reshape(NBLK)
    send = pack(owner, block_cell, features, point_weights, point_corner.reshape(NBLK, NPTS))
    recv = a2a(send, ("row", "col"))
    field, zs, ids = scatter(recv, tz)
    zs = a2a(zs, "col")
    ys = y_forward(zs, ty)
    ys = a2a(ys, "row")
    xs = x_mix(ys, spec_weight, tx, ix)
    xs = a2a(xs, "row")
    yi = y_inverse(xs, iy)
    yi = a2a(yi, "col")
    vals = final(ids, yi, field, recv, iz, w1, b1, w2)
    vals = a2a(vals, ("row", "col"))
    return unpack(owner, vals)


def solution(mesh):
    return jax.shard_map(
        body,
        mesh=mesh,
        in_specs=(
            P(None, ("row", "col")),
            P(None, ("row", "col")),
            P(("row", "col")),
            P(("row", "col"), None),
            P(("row", "col")),
            P("col", "row", None, None, None),
            P(),
            P(),
            P(),
            P(),
        ),
        out_specs=P(None, ("row", "col")),
        check_vma=False,
    )
```

```python
import math
from functools import partial

import jax
import jax.numpy as jnp
import numpy as np
from jax import lax
from jax.experimental import pallas as pl
from jax.experimental.pallas import tpu as pltpu
from jax.sharding import PartitionSpec as P

GRID = 256
MODES = 64
BE = 8
NPTS = 128
NBLK = 128
NSLOT = 256
ROWS = 8
COLS = 16
CH = 16
HID = 64
F32 = jnp.float32
BF16 = jnp.bfloat16
NN = (((1,), (0,)), ((), ()))
NT = (((1,), (1,)), ((), ()))
TN = (((0,), (0,)), ((), ()))


def mm(a, b, dims=NN):
    return lax.dot_general(a, b, dims, preferred_element_type=F32)


def _freqs():
    j = np.arange(MODES)
    return np.where(j < MODES // 2, j, GRID - MODES + j)


def _trig(freq):
    turns = (np.arange(GRID)[:, None] * freq[None, :]) % GRID
    theta = (2.0 * math.pi / GRID) * turns
    f = 1.0 / math.sqrt(GRID)
    return np.cos(theta) * f, np.sin(theta) * f


def tables():
    cz, sz = _trig(np.arange(MODES))
    cf, sf = _trig(_freqs())
    tz = np.stack([cz, -sz], -1).reshape(GRID, 2 * MODES).T
    fwd = np.stack([np.stack([cf, -sf], -1), np.stack([sf, cf], -1)], 1)
    inv = np.stack(
        [np.stack([cf.T, sf.T], -1), np.stack([-sf.T, cf.T], -1)], 1
    )
    ty = fwd.reshape(COLS, 16, 2, 4, 16, 2).transpose(3, 5, 4, 0, 2, 1).reshape(128, 512)
    tx = fwd.reshape(ROWS, 2, 2, 8, 2, MODES, 2).transpose(6, 5, 0, 1, 4, 2, 3).reshape(128, 512)
    ix = inv.reshape(MODES, 2, ROWS, 2, 2, 8, 2).transpose(2, 3, 6, 4, 5, 1, 0).reshape(512, 128)
    iy = inv.reshape(4, 16, 2, COLS, 16, 2).transpose(3, 5, 4, 0, 2, 1).reshape(512, 128)
    a = np.where(np.arange(MODES) == 0, 1.0, 2.0)[None, :]
    iz = np.stack([a * cz, -a * sz], -1).reshape(GRID, 2 * MODES)
    return [jnp.asarray(t.astype(np.float32)).astype(BF16) for t in (tz, ty, tx, ix, iy, iz)]


def div_const(v, d):
    return ((v.astype(F32) + 0.5) * (1.0 / d)).astype(jnp.int32)


def pack_kernel(own_ref, cell_ref, feat_ref, w_ref, corner_ref, send_ref, cnt_ref):
    zero = jnp.zeros((8, 32, NPTS), BF16)

    @pl.loop(0, NSLOT // 8)
    def _(i):
        send_ref[pl.ds(i * 8, 8)] = zero

    @pl.loop(0, NBLK, unroll=16)
    def _(i):
        cnt_ref[i] = 0

    row = lax.broadcasted_iota(jnp.int32, (8, NPTS), 0)

    @pl.loop(0, NBLK, unroll=8)
    def _(b):
        o = own_ref[b]
        r = cnt_ref[o]
        cnt_ref[o] = r + 1
        slot = o * 2 + jnp.minimum(r, 1)
        at = pl.multiple_of(b * NPTS, NPTS)
        v = jnp.broadcast_to(corner_ref[pl.ds(b, 1), :], (8, NPTS))
        vx = div_const(v, 49)
        rest = v - vx * 49
        vy = div_const(rest, 7)
        vz = rest - vy * 7
        head = jnp.where(
            row == 0, vx, jnp.where(row == 1, vy, jnp.where(row == 2, vz, cell_ref[b] + 1))
        )
        tail = jnp.concatenate([w_ref[:, pl.ds(at, NPTS)].astype(F32), head.astype(F32)], 0)
        send_ref[slot, 0:16, :] = feat_ref[:, pl.ds(at, NPTS)]
        send_ref[slot, 16:32, :] = tail.astype(BF16)


def pack(owner, cell, features, weights, corner):
    smem = pl.BlockSpec(memory_space=pltpu.SMEM)
    vmem = pl.BlockSpec(memory_space=pltpu.VMEM)
    return pl.pallas_call(
        pack_kernel,
        out_shape=jax.ShapeDtypeStruct((NSLOT, 32, NPTS), BF16),
        in_specs=[smem, smem, vmem, vmem, vmem],
        out_specs=vmem,
        scratch_shapes=[pltpu.SMEM((NBLK,), jnp.int32)],
        name="pack",
    )(owner, cell, features, weights, corner)


def yz_basis(tail):
    zi = lax.broadcasted_iota(jnp.int32, (8, NPTS), 0).astype(F32)
    bc = lambda k: jnp.broadcast_to(tail[k : k + 1, :], (8, NPTS))
    vy, vz = bc(9), bc(10)
    m0 = zi == vz
    m1 = zi == vz + 1.0
    zero = jnp.zeros((8, NPTS), F32)
    zc = [
        [
            jnp.where(m0, bc(4 * dx + 2 * dy), jnp.where(m1, bc(4 * dx + 2 * dy + 1), zero))
            for dy in range(2)
        ]
        for dx in range(2)
    ]
    my = [vy == float(y) for y in range(7)]
    halves = []
    for dx in range(2):
        rows = []
        for y in range(8):
            val = zero
            if y > 0:
                val = jnp.where(my[y - 1], zc[dx][1], val)
            if y < 7:
                val = jnp.where(my[y], zc[dx][0], val)
            rows.append(val)
        halves.append(jnp.concatenate(rows, 0).astype(BF16))
    return jnp.concatenate(halves, 1)


def split_lanes(a, b):
    low = lax.broadcasted_iota(jnp.int32, a.shape, a.ndim - 1) < 64
    first = jnp.where(low, a, pltpu.roll(b, 64, a.ndim - 1))
    second = jnp.where(low, pltpu.roll(a, 64, a.ndim - 1), b)
    return first, second


def scatter_kernel(
    recv_hbm, tz_ref, field_hbm, out_hbm, ids_ref,
    recv_ref, g_ref, z_ref, field_ref, out_ref, in_sem, field_sem, out_sem, *, unroll
):
    part = NSLOT // 4

    def fetch(k):
        at = pl.ds(k * part, part)
        return pltpu.make_async_copy(recv_hbm.at[at], recv_ref.at[at], in_sem.at[k])

    for k in range(4):
        fetch(k).start()
    zero = jnp.zeros((4, 64, 128), F32)

    @pl.loop(0, 64)
    def _(i):
        g_ref[pl.ds(i * 4, 4)] = zero

    @pl.loop(0, 4)
    def _(k):
        fetch(k).wait()

        @pl.loop(0, part // unroll)
        def _(i):
            for u in range(unroll):
                s = k * part + i * unroll + u
                tail = recv_ref[s, 16:32, :].astype(F32)
                basis = yz_basis(tail)
                feat = recv_ref[s, 0:16, :].astype(F32)
                vx = jnp.broadcast_to(tail[8:9, :], (8, NPTS))
                zf = jnp.zeros((8, NPTS), F32)
                low, high = [], []
                for ch in range(2):
                    half = feat[ch * 8 : ch * 8 + 8]
                    sel = [jnp.where(vx == float(x), half, 0.0) for x in range(7)]
                    low += sel + [zf]
                    high += [zf] + sel
                lhs = jnp.concatenate(
                    [jnp.concatenate(low, 0).astype(BF16), jnp.concatenate(high, 0).astype(BF16)],
                    1,
                )
                res = mm(basis, lhs, NT)
                b = jnp.clip(tail[11, 0].astype(jnp.int32) - 1, 0, 255)
                ids_ref[s] = b
                g_ref[b] = g_ref[b] + res

    tz = tz_ref[...]

    def put_field(q):
        at = pl.ds(q * 8, 8)
        return pltpu.make_async_copy(field_ref.at[at], field_hbm.at[at], field_sem.at[q])

    def put_out(s, r):
        return pltpu.make_async_copy(
            out_ref.at[s, r], out_hbm.at[r * COLS + s], out_sem.at[s, r]
        )

    @pl.loop(0, 8)
    def _(q):
        bx = q // 2
        by = q % 2
        for h in range(4):
            ms = []
            for yl in (2 * h, 2 * h + 1):
                m = g_ref[pl.ds(q * 32, 32), yl * 8 : yl * 8 + 8, :].reshape(GRID, 128)
                m = m.astype(BF16)
                field_ref[q * 8 + yl] = m
                ms.append(m)
            res = mm(tz, jnp.concatenate(ms, 1))
            for e in range(2):
                y = by * 8 + 2 * h + e
                z_ref[bx, pl.ds(y, 128, stride=16), :] = res[:, e * 128 : e * 128 + 128]
        put_field(q).start()

    @pl.loop(0, 16)
    def _(s):
        for kz in range(4):
            for ri in range(2):
                at = pl.multiple_of(s * 128 + kz * 32 + ri * 16, 16)
                for p in range(2):
                    pair = split_lanes(
                        z_ref[2 * p, pl.ds(at, 16), :], z_ref[2 * p + 1, pl.ds(at, 16), :]
                    )
                    for ch in range(2):
                        out_ref[s, 2 * kz + ch, ri, p] = pair[ch].astype(BF16)
        for r in range(8):
            put_out(s, r).start()

    @pl.loop(0, 8)
    def _(q):
        put_field(q).wait()

    @pl.loop(0, 16)
    def _(s):
        for r in range(8):
            put_out(s, r).wait()


def scatter(recv, tz):
    smem = pl.BlockSpec(memory_space=pltpu.SMEM)
    vmem = pl.BlockSpec(memory_space=pltpu.VMEM)
    hbm = pl.BlockSpec(memory_space=pl.ANY)
    return pl.pallas_call(
        partial(scatter_kernel, unroll=16),
        out_shape=(
            jax.ShapeDtypeStruct((64, GRID, 128), BF16),
            jax.ShapeDtypeStruct((128, 2, 2, 16, 128), BF16),
            jax.ShapeDtypeStruct((NSLOT,), jnp.int32),
        ),
        in_specs=[hbm, vmem],
        out_specs=(hbm, hbm, smem),
        scratch_shapes=[
            pltpu.VMEM((NSLOT, 32, NPTS), BF16),
            pltpu.VMEM((256, 64, 128), F32),
            pltpu.VMEM((4, 2048, 128), F32),
            pltpu.VMEM((64, GRID, 128), BF16),
            pltpu.VMEM((16, 8, 2, 2, 16, 128), BF16),
            pltpu.SemaphoreType.DMA((4,)),
            pltpu.SemaphoreType.DMA((8,)),
            pltpu.SemaphoreType.DMA((16, 8)),
        ],
        name="scatter_z",
    )(recv, tz)


def group_transpose(x):
    n = x.shape[0]
    low, high = split_lanes(x[:, 0:8], x[:, 8:16])
    x = jnp.concatenate([low, high], 0)
    si = lax.broadcasted_iota(jnp.int32, x.shape, 1)
    gi = lax.broadcasted_iota(jnp.int32, x.shape, 2) // 8
    for k in range(3):
        d = 1 << k
        mi = (si // d) % 2
        mg = (gi // d) % 2
        up = pltpu.roll(pltpu.roll(x, 8 - d, 1), 8 * d, 2)
        down = pltpu.roll(pltpu.roll(x, d, 1), 128 - 8 * d, 2)
        x = jnp.where(mi == mg, x, jnp.where(mi < mg, up, down))
    return jnp.concatenate([x[:n], x[n:]], 1)


def yx_kernel(in_hbm, ty_ref, tx_ref, out_ref, in_ref, v_ref, sem):
    def get(r):
        at = pl.ds(r * COLS, COLS)
        return pltpu.make_async_copy(in_hbm.at[at], in_ref.at[at], sem.at[r])

    for r in range(8):
        get(r).start()

    @pl.loop(0, 8)
    def _(r):
        get(r).wait()
        at = pl.ds(r * COLS, COLS)
        rhs = jnp.concatenate([in_ref[at, :, p].reshape(512, 128) for p in range(2)], 1)
        res = mm(ty_ref[...], rhs)
        for p in range(2):
            tiles = group_transpose(res[:, p * 128 : p * 128 + 128].reshape(8, 16, 128))
            tiles = tiles.reshape(4, 32, 128).astype(BF16)
            to = pl.multiple_of(r * 64 + p * 32, 32)
            for g in range(4):
                v_ref[g, pl.ds(to, 32), :] = tiles[g]

    for g in range(4):
        spec = mm(tx_ref[...], v_ref[g]).T.astype(BF16)
        out_ref[2 * g] = spec[0:64]
        out_ref[2 * g + 1] = spec[64:128]


def yx_forward(zs, ty, tx):
    vmem = pl.BlockSpec(memory_space=pltpu.VMEM)
    hbm = pl.BlockSpec(memory_space=pl.ANY)
    return pl.pallas_call(
        yx_kernel,
        out_shape=jax.ShapeDtypeStruct((8, 64, 128), BF16),
        in_specs=[hbm, vmem, vmem],
        out_specs=vmem,
        scratch_shapes=[
            pltpu.VMEM((128, 2, 2, 16, 128), BF16),
            pltpu.VMEM((4, 512, 128), BF16),
            pltpu.SemaphoreType.DMA((8,)),
        ],
        name="yx_forward",
    )(zs, ty, tx)


def mix_kernel(in_ref, w_ref, out_ref):
    lane = lax.broadcasted_iota(jnp.int32, (16, 128), 1)
    halves = [[], []]
    spec = [in_ref[ch].astype(F32) for ch in range(2)]
    swapped = [pltpu.roll(x, 64, 1) for x in spec]
    for ky in range(8):
        a1 = jnp.zeros((16, 128), F32)
        a2 = jnp.zeros((16, 128), F32)
        for c in range(CH):
            w = w_ref[0, ky, c].astype(F32)
            at = ky * 8 + c % 8
            a1 = a1 + spec[c // 8][at : at + 1, :] * w
            a2 = a2 + swapped[c // 8][at : at + 1, :] * w
        res = jnp.where(lane < 64, a1 - pltpu.roll(a1, 64, 1), a2 + pltpu.roll(a2, 64, 1))
        for h in range(2):
            halves[h].append(res[h * 8 : h * 8 + 8])
    for h in range(2):
        out_ref[h] = jnp.concatenate(halves[h], 0).astype(BF16)


def mix(spec, weight):
    return pl.pallas_call(
        mix_kernel,
        grid=(4,),
        out_shape=jax.ShapeDtypeStruct((8, 64, 128), BF16),
        in_specs=[
            pl.BlockSpec((2, 64, 128), lambda k: (k, 0, 0)),
            pl.BlockSpec((1, 8, 16, 16, 128), lambda k: (k, 0, 0, 0, 0)),
        ],
        out_specs=pl.BlockSpec((2, 64, 128), lambda k: (k, 0, 0)),
        name="mix",
    )(spec, weight)


def xy_kernel(in_ref, ix_ref, iy_ref, out_hbm, u_ref, out_ref, sem):
    def put(r):
        at = pl.ds(r * COLS, COLS)
        return pltpu.make_async_copy(out_ref.at[at], out_hbm.at[at], sem.at[r])

    @pl.loop(0, 4)
    def _(g):
        rhs = in_ref[pl.ds(2 * g, 2)].reshape(128, 128)
        xi = group_transpose(mm(ix_ref[...], rhs, NT).reshape(32, 16, 128))
        u_ref[g] = xi.astype(BF16)

    @pl.loop(0, 8)
    def _(r):
        rhs = jnp.concatenate(
            [u_ref[:, pl.ds(r * 4 + p * 2, 2)].reshape(128, 128) for p in range(2)], 1
        )
        res = mm(iy_ref[...], rhs).astype(BF16)
        for s in range(16):
            for ri in range(2):
                at = s * 32 + ri * 16
                for p in range(2):
                    out_ref[r * COLS + s, ri, p] = res[at : at + 16, p * 128 : p * 128 + 128]
        put(r).start()

    for r in range(8):
        put(r).wait()


def xy_inverse(mixed, ix, iy):
    vmem = pl.BlockSpec(memory_space=pltpu.VMEM)
    hbm = pl.BlockSpec(memory_space=pl.ANY)
    return pl.pallas_call(
        xy_kernel,
        out_shape=jax.ShapeDtypeStruct((128, 2, 2, 16, 128), BF16),
        in_specs=[vmem, vmem, vmem],
        out_specs=hbm,
        scratch_shapes=[
            pltpu.VMEM((4, 32, 16, 128), BF16),
            pltpu.VMEM((128, 2, 2, 16, 128), BF16),
            pltpu.SemaphoreType.DMA((8,)),
        ],
        name="xy_inverse",
    )(mixed, ix, iy)


def gelu(x):
    x = x.astype(BF16)
    c = math.sqrt(2.0 / math.pi)
    t = jnp.tanh(x * (jnp.asarray(c, BF16) + jnp.asarray(c * 0.044715, BF16) * (x * x)))
    h = x * jnp.asarray(0.5, BF16)
    return h + h * t


def final_kernel(
    ids_ref, yi_hbm, field_hbm, recv_hbm, iz_ref, w1_ref, b1_ref, w2_ref, out_hbm,
    yi_ref, field_ref, tail_ref, out_ref, y_ref, x_ref, l_ref,
    yi_sem, field_sem, tail_sem, out_sem, *, ny, unroll
):
    def get_yi(r):
        at = pl.ds(r * COLS, COLS)
        return pltpu.make_async_copy(yi_hbm.at[at], yi_ref.at[at], yi_sem.at[r])

    def get_field(i):
        at = pl.ds(i * ny, ny)
        return pltpu.make_async_copy(field_hbm.at[at], field_ref.at[at], field_sem.at[i])

    def put_out(i):
        at = pl.ds(i * unroll, unroll)
        return pltpu.make_async_copy(out_ref.at[at], out_hbm.at[at], out_sem.at[i])

    get_tail = pltpu.make_async_copy(recv_hbm.at[:, 16:32], tail_ref, tail_sem)

    @pl.loop(0, 8)
    def _(r):
        get_yi(r).start()

    @pl.loop(0, 64 // ny)
    def _(i):
        get_field(i).start()

    get_tail.start()

    @pl.loop(0, 4)
    def _(kz):
        get_yi(2 * kz).wait()
        get_yi(2 * kz + 1).wait()

        @pl.loop(0, 16)
        def _(s):
            for ri in range(2):
                at = pl.multiple_of(s * 128 + kz * 32 + ri * 16, 16)
                for p in range(2):
                    pair = split_lanes(
                        yi_ref[kz * 32 + s, ri, p].astype(F32),
                        yi_ref[kz * 32 + 16 + s, ri, p].astype(F32),
                    )
                    for e in range(2):
                        y_ref[2 * p + e, pl.ds(at, 16), :] = pair[e]

    @pl.loop(0, 64 // ny)
    def _(i):
        base = i * ny
        bx = base // 16
        get_field(i).wait()
        for p in range(ny // 2):
            y = (base + 2 * p) % 16
            rhs = jnp.concatenate(
                [y_ref[bx, pl.ds(y + e, 128, stride=16), :] for e in range(2)], 1
            ).astype(BF16)
            res = mm(iz_ref[...], rhs).astype(BF16)
            for e in range(2):
                at = (2 * p + e) * GRID
                x_ref[at : at + GRID, 0:128] = res[:, e * 128 : e * 128 + 128]
                x_ref[at : at + GRID, 128:256] = field_ref[base + 2 * p + e]
        h = gelu(mm(x_ref[...], w1_ref[...]) + b1_ref[...])
        o = mm(h, w2_ref[...]).astype(BF16).astype(F32)
        l_ref[pl.ds(base, ny)] = o.reshape(ny, GRID, 128)

    get_tail.wait()

    @pl.loop(0, NSLOT // unroll)
    def _(i):
        for u in range(unroll):
            s = i * unroll + u
            tail = tail_ref[s].astype(F32)
            basis = yz_basis(tail)
            b = ids_ref[s]
            q = b // 32
            at = pl.multiple_of((b % 32) * 8, 8)
            cells = l_ref[pl.ds(q * 8, 8), pl.ds(at, 8), :].reshape(64, 128).astype(BF16)
            res = mm(cells, basis, TN)
            vx = jnp.broadcast_to(tail[8:9, :], (16, NPTS))
            val = jnp.zeros((16, NPTS), F32)
            for x in range(7):
                got = res[x * 16 : x * 16 + 16, 0:128] + res[x * 16 + 16 : x * 16 + 32, 128:256]
                val = jnp.where(vx == float(x), got, val)
            out_ref[s] = val.astype(BF16)
        put_out(i).start()

    @pl.loop(0, NSLOT // unroll)
    def _(i):
        put_out(i).wait()


def final(ids, yi, field, recv, iz, w1, b1, w2):
    smem = pl.BlockSpec(memory_space=pltpu.SMEM)
    vmem = pl.BlockSpec(memory_space=pltpu.VMEM)
    hbm = pl.BlockSpec(memory_space=pl.ANY)
    ny, unroll = 8, 32
    return pl.pallas_call(
        partial(final_kernel, ny=ny, unroll=unroll),
        out_shape=jax.ShapeDtypeStruct((NSLOT, 16, NPTS), BF16),
        in_specs=[smem, hbm, hbm, hbm, vmem, vmem, vmem, vmem],
        out_specs=hbm,
        scratch_shapes=[
            pltpu.VMEM((128, 2, 2, 16, 128), BF16),
            pltpu.VMEM((64, GRID, 128), BF16),
            pltpu.VMEM((NSLOT, 16, NPTS), BF16),
            pltpu.VMEM((NSLOT, 16, NPTS), BF16),
            pltpu.VMEM((4, 2048, 128), F32),
            pltpu.VMEM((ny * GRID, 256), BF16),
            pltpu.VMEM((64, GRID, 128), F32),
            pltpu.SemaphoreType.DMA((8,)),
            pltpu.SemaphoreType.DMA((64 // ny,)),
            pltpu.SemaphoreType.DMA,
            pltpu.SemaphoreType.DMA((NSLOT // unroll,)),
        ],
        name="mlp_gather",
    )(ids, yi, field, recv, iz, w1, b1, w2)


def unpack_kernel(own_ref, in_ref, out_ref, cnt_ref):
    @pl.loop(0, NBLK, unroll=16)
    def _(i):
        cnt_ref[i] = 0

    @pl.loop(0, NBLK, unroll=8)
    def _(b):
        o = own_ref[b]
        r = cnt_ref[o]
        cnt_ref[o] = r + 1
        slot = o * 2 + jnp.minimum(r, 1)
        at = pl.multiple_of(b * NPTS, NPTS)
        out_ref[:, pl.ds(at, NPTS)] = in_ref[slot]


def unpack(owner, vals):
    smem = pl.BlockSpec(memory_space=pltpu.SMEM)
    vmem = pl.BlockSpec(memory_space=pltpu.VMEM)
    return pl.pallas_call(
        unpack_kernel,
        out_shape=jax.ShapeDtypeStruct((CH, NBLK * NPTS), BF16),
        in_specs=[smem, vmem],
        out_specs=vmem,
        scratch_shapes=[pltpu.SMEM((NBLK,), jnp.int32)],
        name="unpack",
    )(owner, vals)


def a2a(x, axes):
    return lax.all_to_all(x, axes, split_axis=0, concat_axis=0, tiled=True)


def body(
    features,
    point_weights,
    point_corner,
    block_owner,
    block_cell,
    spec_weight,
    skip_weight,
    mlp_in,
    mlp_bias,
    mlp_out,
):
    tz, ty, tx, ix, iy, iz = tables()
    eye = jnp.eye(8, dtype=BF16)
    both = jnp.dot(mlp_in, skip_weight, preferred_element_type=F32).astype(BF16)
    w1 = jnp.stack([jnp.kron(eye, mlp_in.T), jnp.kron(eye, both.T)], 0)
    w1 = w1.reshape(2, 8, 2, 8, 512).transpose(0, 2, 1, 3, 4).reshape(256, 512)
    w2 = jnp.kron(eye, mlp_out.T)
    b1 = jnp.tile(mlp_bias, 8)[None, :]
    owner = block_owner.reshape(NBLK)
    send = pack(owner, block_cell, features, point_weights, point_corner.reshape(NBLK, NPTS))
    recv = a2a(send, ("row", "col"))
    field, zs, ids = scatter(recv, tz)
    zs = a2a(zs, ("row", "col"))
    spec = a2a(yx_forward(zs, ty, tx), "row")
    mixed = a2a(mix(spec, spec_weight), "row")
    yi = a2a(xy_inverse(mixed, ix, iy), ("row", "col"))
    vals = final(ids, yi, field, recv, iz, w1, b1, w2)
    vals = a2a(vals, ("row", "col"))
    return unpack(owner, vals)


def solution(mesh):
    return jax.shard_map(
        body,
        mesh=mesh,
        in_specs=(
            P(None, ("row", "col")),
            P(None, ("row", "col")),
            P(("row", "col")),
            P(("row", "col"), None),
            P(("row", "col")),
            P("col", "row", None, None, None),
            P(),
            P(),
            P(),
            P(),
        ),
        out_specs=P(None, ("row", "col")),
        check_vma=False,
    )
```

```python
import math
from functools import partial

import jax
import jax.numpy as jnp
import numpy as np
from jax import lax
from jax.experimental import pallas as pl
from jax.experimental.pallas import tpu as pltpu
from jax.sharding import PartitionSpec as P

GRID = 256
MODES = 64
BE = 8
NPTS = 128
NBLK = 128
NSLOT = 256
ROWS = 8
COLS = 16
CH = 16
HID = 64
F32 = jnp.float32
BF16 = jnp.bfloat16
NN = (((1,), (0,)), ((), ()))
NT = (((1,), (1,)), ((), ()))
TN = (((0,), (0,)), ((), ()))


def mm(a, b, dims=NN):
    return lax.dot_general(a, b, dims, preferred_element_type=F32)


ROW_IN = np.array([2 * lo + hi for hi in range(2) for lo in range(8)])
ROW_OUT = np.array([2 * ((-t) % 8) + v for v in range(2) for t in range(8)])


def _freqs():
    j = np.arange(MODES)
    return np.where(j < MODES // 2, j, GRID - MODES + j)


def _trig(freq):
    turns = (np.arange(GRID)[:, None] * freq[None, :]) % GRID
    theta = (2.0 * math.pi / GRID) * turns
    f = 1.0 / math.sqrt(GRID)
    return np.cos(theta) * f, np.sin(theta) * f


def tables():
    cz, sz = _trig(np.arange(MODES))
    cf, sf = _trig(_freqs())
    tz = np.stack([cz, -sz], -1).reshape(GRID, 2 * MODES).T
    fwd = np.stack([np.stack([cf, -sf], -1), np.stack([sf, cf], -1)], 1)
    inv = np.stack(
        [np.stack([cf.T, sf.T], -1), np.stack([-sf.T, cf.T], -1)], 1
    )
    ty = fwd.reshape(COLS, 16, 2, 4, 16, 2)[:, :, :, :, ROW_IN]
    ty = ty.transpose(3, 5, 4, 0, 2, 1).reshape(128, 512)
    tx = fwd.reshape(ROWS, 2, 16, 2, MODES, 2)[:, :, ROW_OUT]
    tx = tx.transpose(5, 4, 0, 1, 3, 2).reshape(128, 512)
    ix = inv.reshape(MODES, 2, ROWS, 2, 16, 2)[:, :, :, :, ROW_IN]
    ix = ix.transpose(2, 3, 5, 4, 1, 0).reshape(512, 128)
    iy = inv.reshape(4, 16, 2, COLS, 16, 2)[:, ROW_OUT]
    iy = iy.transpose(3, 5, 4, 0, 2, 1).reshape(512, 128)
    a = np.where(np.arange(MODES) == 0, 1.0, 2.0)[None, :]
    iz = np.stack([a * cz, -a * sz], -1).reshape(GRID, 2 * MODES)
    return [jnp.asarray(t.astype(np.float32)).astype(BF16) for t in (tz, ty, tx, ix, iy, iz)]


def div_const(v, d):
    return ((v.astype(F32) + 0.5) * (1.0 / d)).astype(jnp.int32)


def pack_kernel(
    own_ref, cell_ref, feat_ref, w_ref, corner_ref, send_ref, slot_ref, cnt_ref, head_ref
):
    zero = jnp.zeros((8, 56, NPTS), BF16)

    @pl.loop(0, NBLK // 8)
    def _(i):
        send_ref[pl.ds(i * 8, 8)] = zero
        head_ref[pl.ds(i * 8, 8)] = jnp.zeros((8, 8, NPTS), F32)

    @pl.loop(0, NBLK, unroll=16)
    def _(i):
        cnt_ref[i] = 0

    row = lax.broadcasted_iota(jnp.int32, (4, NPTS), 0)

    @pl.loop(0, NBLK, unroll=8)
    def _(b):
        o = own_ref[b]
        r = cnt_ref[o]
        cnt_ref[o] = r + 1
        r = jnp.minimum(r, 1)
        slot_ref[b] = o * 2 + r
        at = pl.multiple_of(b * NPTS, NPTS)
        v = jnp.broadcast_to(corner_ref[pl.ds(b, 1), :], (4, NPTS))
        vx = div_const(v, 49)
        rest = v - vx * 49
        vy = div_const(rest, 7)
        vz = rest - vy * 7
        head = jnp.where(
            row == 0, vx, jnp.where(row == 1, vy, jnp.where(row == 2, vz, cell_ref[b] + 1))
        )
        send_ref[o, pl.ds(pl.multiple_of(r * 16, 16), 16), :] = feat_ref[:, pl.ds(at, NPTS)]
        send_ref[o, pl.ds(pl.multiple_of(32 + r * 8, 8), 8), :] = w_ref[:, pl.ds(at, NPTS)]
        head_ref[o, pl.ds(r * 4, 4), :] = head.astype(F32)

    @pl.loop(0, NBLK // 8)
    def _(i):
        send_ref[pl.ds(i * 8, 8), 48:56, :] = head_ref[pl.ds(i * 8, 8)].astype(BF16)


def pack(owner, cell, features, weights, corner):
    smem = pl.BlockSpec(memory_space=pltpu.SMEM)
    vmem = pl.BlockSpec(memory_space=pltpu.VMEM)
    return pl.pallas_call(
        pack_kernel,
        out_shape=(
            jax.ShapeDtypeStruct((NBLK, 56, NPTS), BF16),
            jax.ShapeDtypeStruct((NBLK,), jnp.int32),
        ),
        in_specs=[smem, smem, vmem, vmem, vmem],
        out_specs=(vmem, smem),
        scratch_shapes=[pltpu.SMEM((NBLK,), jnp.int32), pltpu.VMEM((NBLK, 8, NPTS), F32)],
        name="pack",
    )(owner, cell, features, weights, corner)


def yz_basis(w, head):
    zi = lax.broadcasted_iota(jnp.int32, (8, NPTS), 0).astype(F32)
    bc = lambda k: jnp.broadcast_to(w[k : k + 1, :], (8, NPTS))
    vy = jnp.broadcast_to(head[1:2, :], (8, NPTS))
    vz = jnp.broadcast_to(head[2:3, :], (8, NPTS))
    m0 = zi == vz
    m1 = zi == vz + 1.0
    zero = jnp.zeros((8, NPTS), F32)
    zc = [
        [
            jnp.where(m0, bc(4 * dx + 2 * dy), jnp.where(m1, bc(4 * dx + 2 * dy + 1), zero))
            for dy in range(2)
        ]
        for dx in range(2)
    ]
    my = [vy == float(y) for y in range(7)]
    halves = []
    for dx in range(2):
        rows = []
        for y in range(8):
            val = zero
            if y > 0:
                val = jnp.where(my[y - 1], zc[dx][1], val)
            if y < 7:
                val = jnp.where(my[y], zc[dx][0], val)
            rows.append(val)
        halves.append(jnp.concatenate(rows, 0).astype(BF16))
    return jnp.concatenate(halves, 1)


def split_lanes(a, b):
    low = lax.broadcasted_iota(jnp.int32, a.shape, a.ndim - 1) < 64
    first = jnp.where(low, a, pltpu.roll(b, 64, a.ndim - 1))
    second = jnp.where(low, pltpu.roll(a, 64, a.ndim - 1), b)
    return first, second


def scatter_kernel(
    recv_hbm, tz_ref, field_hbm, out_hbm, ids_ref,
    recv_ref, g_ref, z_ref, field_ref, out_ref, in_sem, field_sem, out_sem, *, unroll
):
    part = NBLK // 4

    def fetch(k):
        at = pl.ds(k * part, part)
        return pltpu.make_async_copy(recv_hbm.at[at], recv_ref.at[at], in_sem.at[k])

    for k in range(4):
        fetch(k).start()
    zero = jnp.zeros((4, 64, 128), F32)

    @pl.loop(0, 64)
    def _(i):
        g_ref[pl.ds(i * 4, 4)] = zero

    @pl.loop(0, 4)
    def _(k):
        fetch(k).wait()

        @pl.loop(0, part // unroll)
        def _(i):
            for u in range(unroll):
                d = k * part + i * unroll + u
                weights = recv_ref[d, 32:48, :].astype(F32)
                heads = recv_ref[d, 48:56, :].astype(F32)
                for j in range(2):
                    head = heads[4 * j : 4 * j + 4]
                    basis = yz_basis(weights[8 * j : 8 * j + 8], head)
                    feat = recv_ref[d, 16 * j : 16 * j + 16, :].astype(F32)
                    vx = jnp.broadcast_to(head[0:1, :], (8, NPTS))
                    zf = jnp.zeros((8, NPTS), F32)
                    low, high = [], []
                    for ch in range(2):
                        half = feat[ch * 8 : ch * 8 + 8]
                        sel = [jnp.where(vx == float(x), half, 0.0) for x in range(7)]
                        low += sel + [zf]
                        high += [zf] + sel
                    lhs = jnp.concatenate(
                        [
                            jnp.concatenate(low, 0).astype(BF16),
                            jnp.concatenate(high, 0).astype(BF16),
                        ],
                        1,
                    )
                    res = mm(basis, lhs, NT)
                    b = jnp.clip(head[3, 0].astype(jnp.int32) - 1, 0, 255)
                    ids_ref[2 * d + j] = b
                    g_ref[b] = g_ref[b] + res

    tz = tz_ref[...]

    def put_field(q):
        at = pl.ds(q * 8, 8)
        return pltpu.make_async_copy(field_ref.at[at], field_hbm.at[at], field_sem.at[q])

    def put_out(s):
        return pltpu.make_async_copy(out_ref.at[s], out_hbm.at[:, s], out_sem.at[s])

    @pl.loop(0, 8, unroll=2)
    def _(q):
        bx = q // 2
        by = q % 2
        for h in range(4):
            ms = []
            for yl in (2 * h, 2 * h + 1):
                m = g_ref[pl.ds(q * 32, 32), yl * 8 : yl * 8 + 8, :].reshape(GRID, 128)
                m = m.astype(BF16)
                field_ref[q * 8 + yl] = m
                ms.append(m)
            res = mm(tz, jnp.concatenate(ms, 1))
            for e in range(2):
                y = by * 8 + 2 * h + e
                z_ref[bx, pl.ds(y, 128, stride=16), :] = res[:, e * 128 : e * 128 + 128]
        put_field(q).start()

    @pl.loop(0, 16, unroll=4)
    def _(s):
        for kz in range(4):
            for ri in range(2):
                at = pl.multiple_of(s * 128 + kz * 32 + ri * 16, 16)
                for p in range(2):
                    pair = split_lanes(
                        z_ref[2 * p, pl.ds(at, 16), :], z_ref[2 * p + 1, pl.ds(at, 16), :]
                    )
                    for ch in range(2):
                        out_ref[s, 2 * kz + ch, ri, p] = pair[ch].astype(BF16)
        put_out(s).start()

    @pl.loop(0, 8)
    def _(q):
        put_field(q).wait()

    @pl.loop(0, 16)
    def _(s):
        put_out(s).wait()


def scatter(recv, tz):
    smem = pl.BlockSpec(memory_space=pltpu.SMEM)
    vmem = pl.BlockSpec(memory_space=pltpu.VMEM)
    hbm = pl.BlockSpec(memory_space=pl.ANY)
    return pl.pallas_call(
        partial(scatter_kernel, unroll=16),
        out_shape=(
            jax.ShapeDtypeStruct((64, GRID, 128), BF16),
            jax.ShapeDtypeStruct((8, 16, 2, 2, 16, 128), BF16),
            jax.ShapeDtypeStruct((NSLOT,), jnp.int32),
        ),
        in_specs=[hbm, vmem],
        out_specs=(hbm, hbm, smem),
        scratch_shapes=[
            pltpu.VMEM((NBLK, 56, NPTS), BF16),
            pltpu.VMEM((256, 64, 128), F32),
            pltpu.VMEM((4, 2048, 128), F32),
            pltpu.VMEM((64, GRID, 128), BF16),
            pltpu.VMEM((16, 8, 2, 2, 16, 128), BF16),
            pltpu.SemaphoreType.DMA((4,)),
            pltpu.SemaphoreType.DMA((8,)),
            pltpu.SemaphoreType.DMA((16,)),
        ],
        name="scatter_z",
    )(recv, tz)


def group_transpose(x):
    n = x.shape[0]
    low, high = x[:, 0:8], x[:, 8:16]
    even = (lax.broadcasted_iota(jnp.int32, low.shape, 2) // 8) % 2 == 0
    first = jnp.where(even, low, pltpu.roll(high, 8, 2))
    second = jnp.where(even, pltpu.roll(low, 120, 2), high)
    x = jnp.concatenate([first, second], 0)
    group = lax.broadcasted_iota(jnp.int32, x.shape, 2) // 16
    x = pltpu.roll(x, 0, 2, stride=16, stride_axis=1)
    for k in range(3):
        d = 1 << k
        x = jnp.where((group // d) % 2 == 1, pltpu.roll(x, 8 - d, 1), x)
    x = pltpu.roll(x, 0, 2, stride=16, stride_axis=1)
    return jnp.concatenate([x[:n], x[n:]], 1)


def yx_kernel(in_hbm, ty_ref, tx_ref, out_ref, in_ref, v_ref, sem):
    def get(r):
        at = pl.ds(r * COLS, COLS)
        return pltpu.make_async_copy(in_hbm.at[at], in_ref.at[at], sem.at[r])

    for r in range(8):
        get(r).start()

    @pl.loop(0, 8, unroll=2)
    def _(r):
        get(r).wait()
        at = pl.ds(r * COLS, COLS)
        rhs = jnp.concatenate([in_ref[at, :, p].reshape(512, 128) for p in range(2)], 1)
        res = mm(ty_ref[...], rhs)
        for p in range(2):
            tiles = group_transpose(res[:, p * 128 : p * 128 + 128].reshape(8, 16, 128))
            tiles = tiles.reshape(4, 32, 128).astype(BF16)
            to = pl.multiple_of(r * 64 + p * 32, 32)
            for g in range(4):
                v_ref[g, pl.ds(to, 32), :] = tiles[g]

    for g in range(4):
        spec = mm(tx_ref[...], v_ref[g]).T.astype(BF16)
        out_ref[2 * g] = spec[0:64]
        out_ref[2 * g + 1] = spec[64:128]


def yx_forward(zs, ty, tx):
    vmem = pl.BlockSpec(memory_space=pltpu.VMEM)
    hbm = pl.BlockSpec(memory_space=pl.ANY)
    return pl.pallas_call(
        yx_kernel,
        out_shape=jax.ShapeDtypeStruct((8, 64, 128), BF16),
        in_specs=[hbm, vmem, vmem],
        out_specs=vmem,
        scratch_shapes=[
            pltpu.VMEM((128, 2, 2, 16, 128), BF16),
            pltpu.VMEM((4, 512, 128), BF16),
            pltpu.SemaphoreType.DMA((8,)),
        ],
        name="yx_forward",
    )(zs, ty, tx)


def mix_kernel(in_ref, w_ref, out_ref):
    lane = lax.broadcasted_iota(jnp.int32, (16, 128), 1)
    halves = [[], []]
    spec = [in_ref[ch].astype(F32) for ch in range(2)]
    swapped = [pltpu.roll(x, 64, 1) for x in spec]
    for ky in range(8):
        a1 = jnp.zeros((16, 128), F32)
        a2 = jnp.zeros((16, 128), F32)
        for c in range(CH):
            w = w_ref[0, ky, c].astype(F32)
            at = ky * 8 + c % 8
            a1 = a1 + spec[c // 8][at : at + 1, :] * w
            a2 = a2 + swapped[c // 8][at : at + 1, :] * w
        res = jnp.where(lane < 64, a1 - pltpu.roll(a1, 64, 1), a2 + pltpu.roll(a2, 64, 1))
        for h in range(2):
            halves[h].append(res[h * 8 : h * 8 + 8])
    for h in range(2):
        out_ref[h] = jnp.concatenate(halves[h], 0).astype(BF16)


def mix(spec, weight):
    return pl.pallas_call(
        mix_kernel,
        grid=(4,),
        out_shape=jax.ShapeDtypeStruct((8, 64, 128), BF16),
        in_specs=[
            pl.BlockSpec((2, 64, 128), lambda k: (k, 0, 0)),
            pl.BlockSpec((1, 8, 16, 16, 128), lambda k: (k, 0, 0, 0, 0)),
        ],
        out_specs=pl.BlockSpec((2, 64, 128), lambda k: (k, 0, 0)),
        name="mix",
    )(spec, weight)


def xy_kernel(in_ref, ix_ref, iy_ref, out_hbm, u_ref, out_ref, sem):
    def put(r):
        at = pl.ds(r * COLS, COLS)
        return pltpu.make_async_copy(out_ref.at[at], out_hbm.at[at], sem.at[r])

    @pl.loop(0, 4, unroll=2)
    def _(g):
        rhs = in_ref[pl.ds(2 * g, 2)].reshape(128, 128)
        xi = group_transpose(mm(ix_ref[...], rhs, NT).reshape(32, 16, 128))
        u_ref[g] = xi.astype(BF16)

    @pl.loop(0, 8, unroll=2)
    def _(r):
        rhs = jnp.concatenate(
            [u_ref[:, pl.ds(r * 4 + p * 2, 2)].reshape(128, 128) for p in range(2)], 1
        )
        res = mm(iy_ref[...], rhs).astype(BF16)
        for s in range(16):
            for ri in range(2):
                at = s * 32 + ri * 16
                for p in range(2):
                    out_ref[r * COLS + s, ri, p] = res[at : at + 16, p * 128 : p * 128 + 128]
        put(r).start()

    for r in range(8):
        put(r).wait()


def xy_inverse(mixed, ix, iy):
    vmem = pl.BlockSpec(memory_space=pltpu.VMEM)
    hbm = pl.BlockSpec(memory_space=pl.ANY)
    return pl.pallas_call(
        xy_kernel,
        out_shape=jax.ShapeDtypeStruct((128, 2, 2, 16, 128), BF16),
        in_specs=[vmem, vmem, vmem],
        out_specs=hbm,
        scratch_shapes=[
            pltpu.VMEM((4, 32, 16, 128), BF16),
            pltpu.VMEM((128, 2, 2, 16, 128), BF16),
            pltpu.SemaphoreType.DMA((8,)),
        ],
        name="xy_inverse",
    )(mixed, ix, iy)


def gelu(x):
    x = x.astype(BF16)
    c = math.sqrt(2.0 / math.pi)
    t = jnp.tanh(x * (jnp.asarray(c, BF16) + jnp.asarray(c * 0.044715, BF16) * (x * x)))
    h = x * jnp.asarray(0.5, BF16)
    return h + h * t


def expand_weights(in_ref, skip_ref, out_ref, w1_ref, w2_ref):
    iota = lambda shape, d: lax.broadcasted_iota(jnp.int32, shape, d)
    hot = lambda cond: jnp.where(cond, 1.0, 0.0).astype(BF16)
    rep = hot(iota((HID, 512), 0) == iota((HID, 512), 1) % HID)
    row = iota((128, CH), 0)
    chan = hot((row // 64) * 8 + row % 8 == iota((128, CH), 1))
    keep = (iota((128, 512), 0) // 8) % 8 == iota((128, 512), 1) // HID
    first = in_ref[...]
    both = mm(skip_ref[...], first, TN).astype(BF16)
    for e, w in enumerate((first, both)):
        full = mm(chan, mm(w, rep).astype(BF16))
        w1_ref[e * 128 : e * 128 + 128, :] = jnp.where(keep, full, 0.0).astype(BF16)
    rows = hot(iota((512, HID), 0) % HID == iota((512, HID), 1))
    cols = hot(iota((CH, 128), 1) % CH == iota((CH, 128), 0))
    full = mm(mm(rows, out_ref[...], NT).astype(BF16), cols)
    keep = iota((512, 128), 0) // HID == iota((512, 128), 1) // CH
    w2_ref[...] = jnp.where(keep, full, 0.0).astype(BF16)


def final_kernel(
    ids_ref, yi_hbm, field_hbm, recv_hbm, iz_ref, in_ref, skip_ref, bias_ref, mout_ref, out_hbm,
    yi_ref, field_ref, tail_ref, out_ref, y_ref, xa_ref, xb_ref, l_ref, w1_ref, w2_ref, b1_ref,
    yi_sem, field_sem, tail_sem, out_sem, *, ny, unroll
):
    def get_yi(r):
        at = pl.ds(r * COLS, COLS)
        return pltpu.make_async_copy(yi_hbm.at[at], yi_ref.at[at], yi_sem.at[r])

    def put_out(i):
        at = pl.ds(i * 2 * unroll, 2 * unroll)
        return pltpu.make_async_copy(out_ref.at[at], out_hbm.at[at], out_sem.at[i])

    get_field = pltpu.make_async_copy(field_hbm, field_ref, field_sem)
    get_tail = pltpu.make_async_copy(recv_hbm.at[:, 32:56], tail_ref, tail_sem)

    @pl.loop(0, 8)
    def _(r):
        get_yi(r).start()

    get_field.start()
    get_tail.start()
    expand_weights(in_ref, skip_ref, mout_ref, w1_ref, w2_ref)
    b1_ref[...] = jnp.concatenate([bias_ref[...]] * 8, 1)

    @pl.loop(0, 4)
    def _(kz):
        get_yi(2 * kz).wait()
        get_yi(2 * kz + 1).wait()

        @pl.loop(0, 16, unroll=4)
        def _(s):
            for ri in range(2):
                at = pl.multiple_of(s * 128 + kz * 32 + ri * 16, 16)
                for p in range(2):
                    pair = split_lanes(
                        yi_ref[kz * 32 + s, ri, p].astype(F32),
                        yi_ref[kz * 32 + 16 + s, ri, p].astype(F32),
                    )
                    for e in range(2):
                        y_ref[2 * p + e, pl.ds(at, 16), :] = pair[e]

    def stage(i, x_ref):
        base = i * ny
        bx = base // 16
        for p in range(ny // 2):
            y = (base + 2 * p) % 16
            rhs = jnp.concatenate(
                [y_ref[bx, pl.ds(y + e, 128, stride=16), :] for e in range(2)], 1
            ).astype(BF16)
            res = mm(iz_ref[...], rhs).astype(BF16)
            for e in range(2):
                at = (2 * p + e) * GRID
                x_ref[at : at + GRID, 0:128] = res[:, e * 128 : e * 128 + 128]
                x_ref[at : at + GRID, 128:256] = field_ref[base + 2 * p + e]

    def layer(i, x_ref):
        h = gelu(mm(x_ref[...], w1_ref[...]) + b1_ref[...])
        o = mm(h, w2_ref[...]).astype(BF16).astype(F32)
        l_ref[pl.ds(i * ny, ny)] = o.reshape(ny, GRID, 128)

    steps = 64 // ny
    get_field.wait()
    stage(0, xa_ref)

    @pl.loop(0, steps // 2)
    def _(i):
        stage(2 * i + 1, xb_ref)
        layer(2 * i, xa_ref)
        stage(jnp.minimum(2 * i + 2, steps - 1), xa_ref)
        layer(2 * i + 1, xb_ref)

    get_tail.wait()

    @pl.loop(0, NBLK // unroll)
    def _(i):
        for u in range(unroll):
            d = i * unroll + u
            weights = tail_ref[d, 0:16, :].astype(F32)
            heads = tail_ref[d, 16:24, :].astype(F32)
            for j in range(2):
                head = heads[4 * j : 4 * j + 4]
                basis = yz_basis(weights[8 * j : 8 * j + 8], head)
                b = ids_ref[2 * d + j]
                q = b // 32
                at = pl.multiple_of((b % 32) * 8, 8)
                cells = l_ref[pl.ds(q * 8, 8), pl.ds(at, 8), :].reshape(64, 128).astype(BF16)
                res = mm(cells, basis, TN)
                vx = jnp.broadcast_to(head[0:1, :], (16, NPTS))
                val = jnp.zeros((16, NPTS), F32)
                for x in range(7):
                    got = (
                        res[x * 16 : x * 16 + 16, 0:128]
                        + res[x * 16 + 16 : x * 16 + 32, 128:256]
                    )
                    val = jnp.where(vx == float(x), got, val)
                out_ref[2 * d + j] = val.astype(BF16)
        put_out(i).start()

    @pl.loop(0, NBLK // unroll)
    def _(i):
        put_out(i).wait()


def final(ids, yi, field, recv, iz, first, skip, bias, mout):
    smem = pl.BlockSpec(memory_space=pltpu.SMEM)
    vmem = pl.BlockSpec(memory_space=pltpu.VMEM)
    hbm = pl.BlockSpec(memory_space=pl.ANY)
    ny, unroll = 8, 16
    return pl.pallas_call(
        partial(final_kernel, ny=ny, unroll=unroll),
        out_shape=jax.ShapeDtypeStruct((NSLOT, 16, NPTS), BF16),
        in_specs=[smem, hbm, hbm, hbm, vmem, vmem, vmem, vmem, vmem],
        out_specs=hbm,
        scratch_shapes=[
            pltpu.VMEM((128, 2, 2, 16, 128), BF16),
            pltpu.VMEM((64, GRID, 128), BF16),
            pltpu.VMEM((NBLK, 24, NPTS), BF16),
            pltpu.VMEM((NSLOT, 16, NPTS), BF16),
            pltpu.VMEM((4, 2048, 128), F32),
            pltpu.VMEM((ny * GRID, 256), BF16),
            pltpu.VMEM((ny * GRID, 256), BF16),
            pltpu.VMEM((64, GRID, 128), F32),
            pltpu.VMEM((256, 512), BF16),
            pltpu.VMEM((512, 128), BF16),
            pltpu.VMEM((1, 512), F32),
            pltpu.SemaphoreType.DMA((8,)),
            pltpu.SemaphoreType.DMA,
            pltpu.SemaphoreType.DMA,
            pltpu.SemaphoreType.DMA((NBLK // unroll,)),
        ],
        name="mlp_gather",
    )(ids, yi, field, recv, iz, first, skip, bias, mout)


def unpack_kernel(slot_ref, in_ref, out_ref):
    @pl.loop(0, NBLK, unroll=8)
    def _(b):
        at = pl.multiple_of(b * NPTS, NPTS)
        out_ref[:, pl.ds(at, NPTS)] = in_ref[slot_ref[b]]


def unpack(slots, vals):
    smem = pl.BlockSpec(memory_space=pltpu.SMEM)
    vmem = pl.BlockSpec(memory_space=pltpu.VMEM)
    return pl.pallas_call(
        unpack_kernel,
        out_shape=jax.ShapeDtypeStruct((CH, NBLK * NPTS), BF16),
        in_specs=[smem, vmem],
        out_specs=vmem,
        name="unpack",
    )(slots, vals)


def a2a(x, axes):
    return lax.all_to_all(x, axes, split_axis=0, concat_axis=0, tiled=True)


def body(
    features,
    point_weights,
    point_corner,
    block_owner,
    block_cell,
    spec_weight,
    skip_weight,
    mlp_in,
    mlp_bias,
    mlp_out,
):
    tz, ty, tx, ix, iy, iz = tables()
    owner = block_owner.reshape(NBLK)
    send, slots = pack(
        owner, block_cell, features, point_weights, point_corner.reshape(NBLK, NPTS)
    )
    recv = a2a(send, ("row", "col"))
    field, zs, ids = scatter(recv, tz)
    zs = a2a(zs.reshape(128, 2, 2, 16, 128), ("row", "col"))
    spec = a2a(yx_forward(zs, ty, tx), "row")
    mixed = a2a(mix(spec, spec_weight), "row")
    yi = a2a(xy_inverse(mixed, ix, iy), ("row", "col"))
    vals = final(
        ids, yi, field, recv, iz, mlp_in.T, skip_weight, mlp_bias.reshape(1, HID), mlp_out
    )
    return unpack(slots, a2a(vals, ("row", "col")))


def solution(mesh):
    return jax.shard_map(
        body,
        mesh=mesh,
        in_specs=(
            P(None, ("row", "col")),
            P(None, ("row", "col")),
            P(("row", "col")),
            P(("row", "col"), None),
            P(("row", "col")),
            P("col", "row", None, None, None),
            P(),
            P(),
            P(),
            P(),
        ),
        out_specs=P(None, ("row", "col")),
        check_vma=False,
    )
```

```python
import math
from functools import partial

import jax
import jax.numpy as jnp
import numpy as np
from jax import lax
from jax.experimental import pallas as pl
from jax.experimental.pallas import tpu as pltpu
from jax.sharding import PartitionSpec as P

GRID = 256
MODES = 64
BE = 8
NPTS = 128
NBLK = 128
NSLOT = 256
ROWS = 8
COLS = 16
CH = 16
HID = 64
F32 = jnp.float32
BF16 = jnp.bfloat16
NN = (((1,), (0,)), ((), ()))
NT = (((1,), (1,)), ((), ()))
TN = (((0,), (0,)), ((), ()))


def mm(a, b, dims=NN):
    return lax.dot_general(a, b, dims, preferred_element_type=F32)


ROW_IN = np.array([2 * lo + hi for hi in range(2) for lo in range(8)])
ROW_OUT = np.array([2 * ((-t) % 8) + v for v in range(2) for t in range(8)])


def _freqs():
    j = np.arange(MODES)
    return np.where(j < MODES // 2, j, GRID - MODES + j)


def _trig(freq):
    turns = (np.arange(GRID)[:, None] * freq[None, :]) % GRID
    theta = (2.0 * math.pi / GRID) * turns
    f = 1.0 / math.sqrt(GRID)
    return np.cos(theta) * f, np.sin(theta) * f


def tables():
    cz, sz = _trig(np.arange(MODES))
    cf, sf = _trig(_freqs())
    tz = np.stack([cz, -sz], -1).reshape(GRID, 2 * MODES).T
    fwd = np.stack([np.stack([cf, -sf], -1), np.stack([sf, cf], -1)], 1)
    inv = np.stack(
        [np.stack([cf.T, sf.T], -1), np.stack([-sf.T, cf.T], -1)], 1
    )
    ty = fwd.reshape(COLS, 16, 2, 4, 16, 2)[:, :, :, :, ROW_IN]
    ty = ty.transpose(3, 5, 4, 0, 2, 1).reshape(128, 512)
    tx = fwd.reshape(ROWS, 2, 16, 2, MODES, 2)[:, :, ROW_OUT]
    tx = tx.transpose(5, 4, 0, 1, 3, 2).reshape(128, 512)
    ix = inv.reshape(MODES, 2, ROWS, 2, 16, 2)[:, :, :, :, ROW_IN]
    ix = ix.transpose(2, 3, 5, 4, 1, 0).reshape(512, 128)
    iy = inv.reshape(4, 16, 2, COLS, 16, 2)[:, ROW_OUT]
    iy = iy.transpose(3, 5, 4, 0, 2, 1).reshape(512, 128)
    a = np.where(np.arange(MODES) == 0, 1.0, 2.0)[None, :]
    iz = np.stack([a * cz, -a * sz], -1).reshape(GRID, 2 * MODES)
    return [jnp.asarray(t.astype(np.float32)).astype(BF16) for t in (tz, ty, tx, ix, iy, iz)]


def div_const(v, d):
    return ((v.astype(F32) + 0.5) * (1.0 / d)).astype(jnp.int32)


def pack_kernel(
    row_ref, own_ref, cell_ref, feat_ref, w_ref, corner_ref, mode_hbm,
    send_ref, slot_ref, m1_hbm, m2_hbm, m3_hbm, cnt_ref, head_ref, sem
):
    chip = row_ref[0] // 2
    copies = [
        pltpu.make_async_copy(mode_hbm.at[(chip + 1 + i) % 4], out, sem.at[i])
        for i, out in enumerate((m1_hbm, m2_hbm, m3_hbm))
    ]
    for copy in copies:
        copy.start()
    zero = jnp.zeros((8, 56, NPTS), BF16)

    @pl.loop(0, NBLK // 8)
    def _(i):
        send_ref[pl.ds(i * 8, 8)] = zero
        head_ref[pl.ds(i * 8, 8)] = jnp.zeros((8, 8, NPTS), F32)

    @pl.loop(0, NBLK, unroll=16)
    def _(i):
        cnt_ref[i] = 0

    row = lax.broadcasted_iota(jnp.int32, (4, NPTS), 0)

    @pl.loop(0, NBLK, unroll=8)
    def _(b):
        o = own_ref[b]
        r = cnt_ref[o]
        cnt_ref[o] = r + 1
        r = jnp.minimum(r, 1)
        slot_ref[b] = o * 2 + r
        at = pl.multiple_of(b * NPTS, NPTS)
        v = jnp.broadcast_to(corner_ref[pl.ds(b, 1), :], (4, NPTS))
        vx = div_const(v, 49)
        rest = v - vx * 49
        vy = div_const(rest, 7)
        vz = rest - vy * 7
        head = jnp.where(
            row == 0, vx, jnp.where(row == 1, vy, jnp.where(row == 2, vz, cell_ref[b] + 1))
        )
        send_ref[o, pl.ds(pl.multiple_of(r * 16, 16), 16), :] = feat_ref[:, pl.ds(at, NPTS)]
        send_ref[o, pl.ds(pl.multiple_of(32 + r * 8, 8), 8), :] = w_ref[:, pl.ds(at, NPTS)]
        head_ref[o, pl.ds(r * 4, 4), :] = head.astype(F32)

    @pl.loop(0, NBLK // 8)
    def _(i):
        send_ref[pl.ds(i * 8, 8), 48:56, :] = head_ref[pl.ds(i * 8, 8)].astype(BF16)

    for copy in copies:
        copy.wait()


def pack(row, owner, cell, features, weights, corner, modes):
    smem = pl.BlockSpec(memory_space=pltpu.SMEM)
    vmem = pl.BlockSpec(memory_space=pltpu.VMEM)
    hbm = pl.BlockSpec(memory_space=pl.ANY)
    part = jax.ShapeDtypeStruct((8, CH, CH, 128), BF16)
    return pl.pallas_call(
        pack_kernel,
        out_shape=(
            jax.ShapeDtypeStruct((NBLK, 56, NPTS), BF16),
            jax.ShapeDtypeStruct((NBLK,), jnp.int32),
            part,
            part,
            part,
        ),
        in_specs=[smem, smem, smem, vmem, vmem, vmem, hbm],
        out_specs=(vmem, smem, hbm, hbm, hbm),
        scratch_shapes=[
            pltpu.SMEM((NBLK,), jnp.int32),
            pltpu.VMEM((NBLK, 8, NPTS), F32),
            pltpu.SemaphoreType.DMA((3,)),
        ],
        name="pack",
    )(row, owner, cell, features, weights, corner, modes)


def yz_basis(w, head):
    zi = lax.broadcasted_iota(jnp.int32, (8, NPTS), 0).astype(F32)
    bc = lambda k: jnp.broadcast_to(w[k : k + 1, :], (8, NPTS))
    vy = jnp.broadcast_to(head[1:2, :], (8, NPTS))
    vz = jnp.broadcast_to(head[2:3, :], (8, NPTS))
    m0 = zi == vz
    m1 = zi == vz + 1.0
    zero = jnp.zeros((8, NPTS), F32)
    zc = [
        [
            jnp.where(m0, bc(4 * dx + 2 * dy), jnp.where(m1, bc(4 * dx + 2 * dy + 1), zero))
            for dy in range(2)
        ]
        for dx in range(2)
    ]
    my = [vy == float(y) for y in range(7)]
    halves = []
    for dx in range(2):
        rows = []
        for y in range(8):
            val = zero
            if y > 0:
                val = jnp.where(my[y - 1], zc[dx][1], val)
            if y < 7:
                val = jnp.where(my[y], zc[dx][0], val)
            rows.append(val)
        halves.append(jnp.concatenate(rows, 0).astype(BF16))
    return jnp.concatenate(halves, 1)


def split_lanes(a, b):
    low = lax.broadcasted_iota(jnp.int32, a.shape, a.ndim - 1) < 64
    first = jnp.where(low, a, pltpu.roll(b, 64, a.ndim - 1))
    second = jnp.where(low, pltpu.roll(a, 64, a.ndim - 1), b)
    return first, second


def scatter_kernel(
    recv_hbm, tz_ref, field_hbm, out_hbm, ids_ref,
    recv_ref, g_ref, z_ref, field_ref, out_ref, in_sem, field_sem, out_sem, *, unroll
):
    part = NBLK // 4

    def fetch(k):
        at = pl.ds(k * part, part)
        return pltpu.make_async_copy(recv_hbm.at[at], recv_ref.at[at], in_sem.at[k])

    for k in range(4):
        fetch(k).start()
    zero = jnp.zeros((4, 64, 128), F32)

    @pl.loop(0, 64)
    def _(i):
        g_ref[pl.ds(i * 4, 4)] = zero

    @pl.loop(0, 4)
    def _(k):
        fetch(k).wait()

        @pl.loop(0, part // unroll)
        def _(i):
            for u in range(unroll):
                d = k * part + i * unroll + u
                weights = recv_ref[d, 32:48, :].astype(F32)
                heads = recv_ref[d, 48:56, :].astype(F32)
                for j in range(2):
                    head = heads[4 * j : 4 * j + 4]
                    basis = yz_basis(weights[8 * j : 8 * j + 8], head)
                    feat = recv_ref[d, 16 * j : 16 * j + 16, :].astype(F32)
                    vx = jnp.broadcast_to(head[0:1, :], (8, NPTS))
                    zf = jnp.zeros((8, NPTS), F32)
                    low, high = [], []
                    for ch in range(2):
                        half = feat[ch * 8 : ch * 8 + 8]
                        sel = [jnp.where(vx == float(x), half, 0.0) for x in range(7)]
                        low += sel + [zf]
                        high += [zf] + sel
                    lhs = jnp.concatenate(
                        [
                            jnp.concatenate(low, 0).astype(BF16),
                            jnp.concatenate(high, 0).astype(BF16),
                        ],
                        1,
                    )
                    res = mm(basis, lhs, NT)
                    b = jnp.clip(head[3, 0].astype(jnp.int32) - 1, 0, 255)
                    ids_ref[2 * d + j] = b
                    g_ref[b] = g_ref[b] + res

    tz = tz_ref[...]

    def put_field(q):
        at = pl.ds(q * 8, 8)
        return pltpu.make_async_copy(field_ref.at[at], field_hbm.at[at], field_sem.at[q])

    def put_out(s):
        return pltpu.make_async_copy(out_ref.at[s], out_hbm.at[:, s], out_sem.at[s])

    @pl.loop(0, 8, unroll=2)
    def _(q):
        bx = q // 2
        by = q % 2
        for h in range(4):
            ms = []
            for yl in (2 * h, 2 * h + 1):
                m = g_ref[pl.ds(q * 32, 32), yl * 8 : yl * 8 + 8, :].reshape(GRID, 128)
                m = m.astype(BF16)
                field_ref[q * 8 + yl] = m
                ms.append(m)
            res = mm(tz, jnp.concatenate(ms, 1))
            for e in range(2):
                y = by * 8 + 2 * h + e
                z_ref[bx, pl.ds(y, 128, stride=16), :] = res[:, e * 128 : e * 128 + 128]
        put_field(q).start()

    @pl.loop(0, 16, unroll=4)
    def _(s):
        for kz in range(4):
            for ri in range(2):
                at = pl.multiple_of(s * 128 + kz * 32 + ri * 16, 16)
                for p in range(2):
                    pair = split_lanes(
                        z_ref[2 * p, pl.ds(at, 16), :], z_ref[2 * p + 1, pl.ds(at, 16), :]
                    )
                    for ch in range(2):
                        out_ref[s, 2 * kz + ch, ri, p] = pair[ch].astype(BF16)
        put_out(s).start()

    @pl.loop(0, 8)
    def _(q):
        put_field(q).wait()

    @pl.loop(0, 16)
    def _(s):
        put_out(s).wait()


def scatter(recv, tz):
    smem = pl.BlockSpec(memory_space=pltpu.SMEM)
    vmem = pl.BlockSpec(memory_space=pltpu.VMEM)
    hbm = pl.BlockSpec(memory_space=pl.ANY)
    return pl.pallas_call(
        partial(scatter_kernel, unroll=16),
        out_shape=(
            jax.ShapeDtypeStruct((64, GRID, 128), BF16),
            jax.ShapeDtypeStruct((8, 16, 2, 2, 16, 128), BF16),
            jax.ShapeDtypeStruct((NSLOT,), jnp.int32),
        ),
        in_specs=[hbm, vmem],
        out_specs=(hbm, hbm, smem),
        scratch_shapes=[
            pltpu.VMEM((NBLK, 56, NPTS), BF16),
            pltpu.VMEM((256, 64, 128), F32),
            pltpu.VMEM((4, 2048, 128), F32),
            pltpu.VMEM((64, GRID, 128), BF16),
            pltpu.VMEM((16, 8, 2, 2, 16, 128), BF16),
            pltpu.SemaphoreType.DMA((4,)),
            pltpu.SemaphoreType.DMA((8,)),
            pltpu.SemaphoreType.DMA((16,)),
        ],
        name="scatter_z",
    )(recv, tz)


def group_transpose(x):
    n = x.shape[0]
    low, high = x[:, 0:8], x[:, 8:16]
    even = (lax.broadcasted_iota(jnp.int32, low.shape, 2) // 8) % 2 == 0
    first = jnp.where(even, low, pltpu.roll(high, 8, 2))
    second = jnp.where(even, pltpu.roll(low, 120, 2), high)
    x = jnp.concatenate([first, second], 0)
    group = lax.broadcasted_iota(jnp.int32, x.shape, 2) // 16
    x = pltpu.roll(x, 0, 2, stride=16, stride_axis=1)
    for k in range(3):
        d = 1 << k
        x = jnp.where((group // d) % 2 == 1, pltpu.roll(x, 8 - d, 1), x)
    x = pltpu.roll(x, 0, 2, stride=16, stride_axis=1)
    return jnp.concatenate([x[:n], x[n:]], 1)


def yx_kernel(row_ref, in_hbm, ty_ref, tx_ref, keep_ref, send_ref, in_ref, v_ref, sem):
    def get(r):
        at = pl.ds(r * COLS, COLS)
        return pltpu.make_async_copy(in_hbm.at[at], in_ref.at[at], sem.at[r])

    for r in range(8):
        get(r).start()

    @pl.loop(0, 8, unroll=2)
    def _(r):
        get(r).wait()
        at = pl.ds(r * COLS, COLS)
        rhs = jnp.concatenate([in_ref[at, :, p].reshape(512, 128) for p in range(2)], 1)
        res = mm(ty_ref[...], rhs)
        for p in range(2):
            tiles = group_transpose(res[:, p * 128 : p * 128 + 128].reshape(8, 16, 128))
            tiles = tiles.reshape(4, 32, 128).astype(BF16)
            to = pl.multiple_of(r * 64 + p * 32, 32)
            for g in range(4):
                v_ref[g, pl.ds(to, 32), :] = tiles[g]

    first = row_ref[0] % 2 == 0
    for g in range(4):
        spec = mm(tx_ref[...], v_ref[g]).T
        keep, send = choose(first, spec[0:64], spec[64:128])
        keep_ref[g] = keep.astype(BF16)
        send_ref[g] = send.astype(BF16)


def choose(first, a, b):
    return jnp.where(first, a, b), jnp.where(first, b, a)


def yx_forward(row, zs, ty, tx):
    smem = pl.BlockSpec(memory_space=pltpu.SMEM)
    vmem = pl.BlockSpec(memory_space=pltpu.VMEM)
    hbm = pl.BlockSpec(memory_space=pl.ANY)
    return pl.pallas_call(
        yx_kernel,
        out_shape=(jax.ShapeDtypeStruct((4, 64, 128), BF16),) * 2,
        in_specs=[smem, hbm, vmem, vmem],
        out_specs=(vmem, vmem),
        scratch_shapes=[
            pltpu.VMEM((128, 2, 2, 16, 128), BF16),
            pltpu.VMEM((4, 512, 128), BF16),
            pltpu.SemaphoreType.DMA((8,)),
        ],
        name="yx_forward",
    )(row, zs, ty, tx)


def mix_kernel(
    row_ref, own_ref, got_ref, mode_hbm, m1_hbm, m2_hbm, m3_hbm, keep_ref, send_ref, w_ref, sem
):
    chip = row_ref[0] // 2
    first = row_ref[0] % 2 == 0
    copies = [
        pltpu.make_async_copy(src, w_ref.at[d], sem.at[d])
        for d, src in enumerate((mode_hbm.at[chip], m1_hbm, m2_hbm, m3_hbm))
    ]
    for copy in copies:
        copy.start()
    lane = lax.broadcasted_iota(jnp.int32, (16, 128), 1)

    for d in range(4):
        copies[d].wait()
        j = (chip + 4 - d) % 4
        spec = choose(first, own_ref[j].astype(F32), got_ref[j].astype(F32))
        swapped = [pltpu.roll(x, 64, 1) for x in spec]
        halves = [[], []]
        for ky in range(8):
            a1 = jnp.zeros((16, 128), F32)
            a2 = jnp.zeros((16, 128), F32)
            for c in range(CH):
                w = w_ref[d, ky, c].astype(F32)
                at = ky * 8 + c % 8
                a1 = a1 + spec[c // 8][at : at + 1, :] * w
                a2 = a2 + swapped[c // 8][at : at + 1, :] * w
            res = jnp.where(lane < 64, a1 - pltpu.roll(a1, 64, 1), a2 + pltpu.roll(a2, 64, 1))
            for h in range(2):
                halves[h].append(res[h * 8 : h * 8 + 8])
        keep, send = choose(first, *[jnp.concatenate(half, 0) for half in halves])
        keep_ref[j] = keep.astype(BF16)
        send_ref[j] = send.astype(BF16)


def mix(row, own, got, modes, parts):
    smem = pl.BlockSpec(memory_space=pltpu.SMEM)
    vmem = pl.BlockSpec(memory_space=pltpu.VMEM)
    hbm = pl.BlockSpec(memory_space=pl.ANY)
    return pl.pallas_call(
        mix_kernel,
        out_shape=(jax.ShapeDtypeStruct((4, 64, 128), BF16),) * 2,
        in_specs=[smem, vmem, vmem, hbm, hbm, hbm, hbm],
        out_specs=(vmem, vmem),
        scratch_shapes=[
            pltpu.VMEM((4, 8, CH, CH, 128), BF16),
            pltpu.SemaphoreType.DMA((4,)),
        ],
        name="mix",
    )(row, own, got, modes, *parts)


def xy_kernel(row_ref, own_ref, got_ref, ix_ref, iy_ref, out_hbm, u_ref, out_ref, sem):
    def put(r):
        at = pl.ds(r * COLS, COLS)
        return pltpu.make_async_copy(out_ref.at[at], out_hbm.at[at], sem.at[r])

    @pl.loop(0, 4, unroll=2)
    def _(g):
        pair = choose(row_ref[0] % 2 == 0, own_ref[g].astype(F32), got_ref[g].astype(F32))
        rhs = jnp.concatenate(pair, 0).astype(BF16)
        xi = group_transpose(mm(ix_ref[...], rhs, NT).reshape(32, 16, 128))
        u_ref[g] = xi.astype(BF16)

    @pl.loop(0, 8, unroll=2)
    def _(r):
        rhs = jnp.concatenate(
            [u_ref[:, pl.ds(r * 4 + p * 2, 2)].reshape(128, 128) for p in range(2)], 1
        )
        res = mm(iy_ref[...], rhs).astype(BF16)
        for s in range(16):
            for ri in range(2):
                at = s * 32 + ri * 16
                for p in range(2):
                    out_ref[r * COLS + s, ri, p] = res[at : at + 16, p * 128 : p * 128 + 128]
        put(r).start()

    for r in range(8):
        put(r).wait()


def xy_inverse(row, own, got, ix, iy):
    smem = pl.BlockSpec(memory_space=pltpu.SMEM)
    vmem = pl.BlockSpec(memory_space=pltpu.VMEM)
    hbm = pl.BlockSpec(memory_space=pl.ANY)
    return pl.pallas_call(
        xy_kernel,
        out_shape=jax.ShapeDtypeStruct((128, 2, 2, 16, 128), BF16),
        in_specs=[smem, vmem, vmem, vmem, vmem],
        out_specs=hbm,
        scratch_shapes=[
            pltpu.VMEM((4, 32, 16, 128), BF16),
            pltpu.VMEM((128, 2, 2, 16, 128), BF16),
            pltpu.SemaphoreType.DMA((8,)),
        ],
        name="xy_inverse",
    )(row, own, got, ix, iy)


def gelu(x):
    x = x.astype(BF16)
    c = math.sqrt(2.0 / math.pi)
    t = jnp.tanh(x * (jnp.asarray(c, BF16) + jnp.asarray(c * 0.044715, BF16) * (x * x)))
    h = x * jnp.asarray(0.5, BF16)
    return h + h * t


def expand_weights(in_ref, skip_ref, out_ref, w1_ref, w2_ref):
    iota = lambda shape, d: lax.broadcasted_iota(jnp.int32, shape, d)
    hot = lambda cond: jnp.where(cond, 1.0, 0.0).astype(BF16)
    rep = hot(iota((HID, 512), 0) == iota((HID, 512), 1) % HID)
    row = iota((128, CH), 0)
    chan = hot((row // 64) * 8 + row % 8 == iota((128, CH), 1))
    keep = (iota((128, 512), 0) // 8) % 8 == iota((128, 512), 1) // HID
    first = in_ref[...]
    both = mm(skip_ref[...], first, TN).astype(BF16)
    for e, w in enumerate((first, both)):
        full = mm(chan, mm(w, rep).astype(BF16))
        w1_ref[e * 128 : e * 128 + 128, :] = jnp.where(keep, full, 0.0).astype(BF16)
    rows = hot(iota((512, HID), 0) % HID == iota((512, HID), 1))
    cols = hot(iota((CH, 128), 1) % CH == iota((CH, 128), 0))
    full = mm(mm(rows, out_ref[...], NT).astype(BF16), cols)
    keep = iota((512, 128), 0) // HID == iota((512, 128), 1) // CH
    w2_ref[...] = jnp.where(keep, full, 0.0).astype(BF16)


def final_kernel(
    ids_ref, yi_hbm, field_hbm, recv_hbm, iz_ref, in_ref, skip_ref, bias_ref, mout_ref, out_hbm,
    yi_ref, field_ref, tail_ref, out_ref, y_ref, xa_ref, xb_ref, l_ref, w1_ref, w2_ref, b1_ref,
    yi_sem, field_sem, tail_sem, out_sem, *, ny, unroll
):
    def get_yi(r):
        at = pl.ds(r * COLS, COLS)
        return pltpu.make_async_copy(yi_hbm.at[at], yi_ref.at[at], yi_sem.at[r])

    def put_out(i):
        at = pl.ds(i * 2 * unroll, 2 * unroll)
        return pltpu.make_async_copy(out_ref.at[at], out_hbm.at[at], out_sem.at[i])

    get_field = pltpu.make_async_copy(field_hbm, field_ref, field_sem)
    get_tail = pltpu.make_async_copy(recv_hbm.at[:, 32:56], tail_ref, tail_sem)

    @pl.loop(0, 8)
    def _(r):
        get_yi(r).start()

    get_field.start()
    get_tail.start()
    expand_weights(in_ref, skip_ref, mout_ref, w1_ref, w2_ref)
    b1_ref[...] = jnp.concatenate([bias_ref[...]] * 8, 1)

    @pl.loop(0, 4)
    def _(kz):
        get_yi(2 * kz).wait()
        get_yi(2 * kz + 1).wait()

        @pl.loop(0, 16, unroll=4)
        def _(s):
            for ri in range(2):
                at = pl.multiple_of(s * 128 + kz * 32 + ri * 16, 16)
                for p in range(2):
                    pair = split_lanes(
                        yi_ref[kz * 32 + s, ri, p].astype(F32),
                        yi_ref[kz * 32 + 16 + s, ri, p].astype(F32),
                    )
                    for e in range(2):
                        y_ref[2 * p + e, pl.ds(at, 16), :] = pair[e]

    def stage(i, x_ref):
        base = i * ny
        bx = base // 16
        for p in range(ny // 2):
            y = (base + 2 * p) % 16
            rhs = jnp.concatenate(
                [y_ref[bx, pl.ds(y + e, 128, stride=16), :] for e in range(2)], 1
            ).astype(BF16)
            res = mm(iz_ref[...], rhs).astype(BF16)
            for e in range(2):
                at = (2 * p + e) * GRID
                x_ref[at : at + GRID, 0:128] = res[:, e * 128 : e * 128 + 128]
                x_ref[at : at + GRID, 128:256] = field_ref[base + 2 * p + e]

    def layer(i, x_ref):
        h = gelu(mm(x_ref[...], w1_ref[...]) + b1_ref[...])
        o = mm(h, w2_ref[...]).astype(BF16).astype(F32)
        l_ref[pl.ds(i * ny, ny)] = o.reshape(ny, GRID, 128)

    steps = 64 // ny
    get_field.wait()
    stage(0, xa_ref)

    @pl.loop(0, steps // 2)
    def _(i):
        stage(2 * i + 1, xb_ref)
        layer(2 * i, xa_ref)
        stage(jnp.minimum(2 * i + 2, steps - 1), xa_ref)
        layer(2 * i + 1, xb_ref)

    get_tail.wait()

    @pl.loop(0, NBLK // unroll)
    def _(i):
        for u in range(unroll):
            d = i * unroll + u
            weights = tail_ref[d, 0:16, :].astype(F32)
            heads = tail_ref[d, 16:24, :].astype(F32)
            for j in range(2):
                head = heads[4 * j : 4 * j + 4]
                basis = yz_basis(weights[8 * j : 8 * j + 8], head)
                b = ids_ref[2 * d + j]
                q = b // 32
                at = pl.multiple_of((b % 32) * 8, 8)
                cells = l_ref[pl.ds(q * 8, 8), pl.ds(at, 8), :].reshape(64, 128).astype(BF16)
                res = mm(cells, basis, TN)
                vx = jnp.broadcast_to(head[0:1, :], (16, NPTS))
                val = jnp.zeros((16, NPTS), F32)
                for x in range(7):
                    got = (
                        res[x * 16 : x * 16 + 16, 0:128]
                        + res[x * 16 + 16 : x * 16 + 32, 128:256]
                    )
                    val = jnp.where(vx == float(x), got, val)
                out_ref[2 * d + j] = val.astype(BF16)
        put_out(i).start()

    @pl.loop(0, NBLK // unroll)
    def _(i):
        put_out(i).wait()


def final(ids, yi, field, recv, iz, first, skip, bias, mout):
    smem = pl.BlockSpec(memory_space=pltpu.SMEM)
    vmem = pl.BlockSpec(memory_space=pltpu.VMEM)
    hbm = pl.BlockSpec(memory_space=pl.ANY)
    ny, unroll = 8, 16
    return pl.pallas_call(
        partial(final_kernel, ny=ny, unroll=unroll),
        out_shape=jax.ShapeDtypeStruct((NSLOT, 16, NPTS), BF16),
        in_specs=[smem, hbm, hbm, hbm, vmem, vmem, vmem, vmem, vmem],
        out_specs=hbm,
        scratch_shapes=[
            pltpu.VMEM((128, 2, 2, 16, 128), BF16),
            pltpu.VMEM((64, GRID, 128), BF16),
            pltpu.VMEM((NBLK, 24, NPTS), BF16),
            pltpu.VMEM((NSLOT, 16, NPTS), BF16),
            pltpu.VMEM((4, 2048, 128), F32),
            pltpu.VMEM((ny * GRID, 256), BF16),
            pltpu.VMEM((ny * GRID, 256), BF16),
            pltpu.VMEM((64, GRID, 128), F32),
            pltpu.VMEM((256, 512), BF16),
            pltpu.VMEM((512, 128), BF16),
            pltpu.VMEM((1, 512), F32),
            pltpu.SemaphoreType.DMA((8,)),
            pltpu.SemaphoreType.DMA,
            pltpu.SemaphoreType.DMA,
            pltpu.SemaphoreType.DMA((NBLK // unroll,)),
        ],
        name="mlp_gather",
    )(ids, yi, field, recv, iz, first, skip, bias, mout)


def unpack_kernel(slot_ref, in_ref, out_ref):
    @pl.loop(0, NBLK, unroll=8)
    def _(b):
        at = pl.multiple_of(b * NPTS, NPTS)
        out_ref[:, pl.ds(at, NPTS)] = in_ref[slot_ref[b]]


def unpack(slots, vals):
    smem = pl.BlockSpec(memory_space=pltpu.SMEM)
    vmem = pl.BlockSpec(memory_space=pltpu.VMEM)
    return pl.pallas_call(
        unpack_kernel,
        out_shape=jax.ShapeDtypeStruct((CH, NBLK * NPTS), BF16),
        in_specs=[smem, vmem],
        out_specs=vmem,
        name="unpack",
    )(slots, vals)


def a2a(x, axes):
    return lax.all_to_all(x, axes, split_axis=0, concat_axis=0, tiled=True)


def partner(x):
    return lax.ppermute(x, "row", [(i, i ^ 1) for i in range(ROWS)])


def body(
    features,
    point_weights,
    point_corner,
    block_owner,
    block_cell,
    spec_weight,
    skip_weight,
    mlp_in,
    mlp_bias,
    mlp_out,
):
    tz, ty, tx, ix, iy, iz = tables()
    owner = block_owner.reshape(NBLK)
    row = lax.axis_index("row").astype(jnp.int32)[None]
    corner = point_corner.reshape(NBLK, NPTS)
    send, slots, *parts = pack(
        row, owner, block_cell, features, point_weights, corner, spec_weight
    )
    parts = [
        lax.ppermute(part, "row", [(i, (i + 2 * d) % ROWS) for i in range(ROWS)])
        for d, part in zip((1, 2, 3), parts)
    ]
    recv = a2a(send, ("row", "col"))
    field, zs, ids = scatter(recv, tz)
    zs = a2a(zs.reshape(128, 2, 2, 16, 128), ("row", "col"))
    keep, send = yx_forward(row, zs, ty, tx)
    keep, send = mix(row, keep, partner(send), spec_weight, parts)
    yi = a2a(xy_inverse(row, keep, partner(send), ix, iy), ("row", "col"))
    vals = final(
        ids, yi, field, recv, iz, mlp_in.T, skip_weight, mlp_bias.reshape(1, HID), mlp_out
    )
    return unpack(slots, a2a(vals, ("row", "col")))


def solution(mesh):
    return jax.shard_map(
        body,
        mesh=mesh,
        in_specs=(
            P(None, ("row", "col")),
            P(None, ("row", "col")),
            P(("row", "col")),
            P(("row", "col"), None),
            P(("row", "col")),
            P("col", "row", None, None, None),
            P(),
            P(),
            P(),
            P(),
        ),
        out_specs=P(None, ("row", "col")),
        check_vma=False,
    )
```

```python
import math
from functools import partial

import jax
import jax.numpy as jnp
import numpy as np
from jax import lax
from jax.experimental import pallas as pl
from jax.experimental.pallas import tpu as pltpu
from jax.sharding import PartitionSpec as P

GRID = 256
MODES = 64
NPTS = 128
NBLK = 128
NSLOT = 256
ROWS = 8
COLS = 16
CH = 16
HID = 64
F32 = jnp.float32
BF16 = jnp.bfloat16
NN = (((1,), (0,)), ((), ()))
NT = (((1,), (1,)), ((), ()))
TN = (((0,), (0,)), ((), ()))


def mm(a, b, dims=NN):
    return lax.dot_general(a, b, dims, preferred_element_type=F32)


ROW_IN = np.array([2 * lo + hi for hi in range(2) for lo in range(8)])
ROW_OUT = np.array([2 * ((-t) % 8) + v for v in range(2) for t in range(8)])


def _freqs():
    j = np.arange(MODES)
    return np.where(j < MODES // 2, j, GRID - MODES + j)


def _trig(freq):
    turns = (np.arange(GRID)[:, None] * freq[None, :]) % GRID
    theta = (2.0 * math.pi / GRID) * turns
    f = 1.0 / math.sqrt(GRID)
    return np.cos(theta) * f, np.sin(theta) * f


def tables():
    cz, sz = _trig(np.arange(MODES))
    cf, sf = _trig(_freqs())
    tz = np.stack([cz, -sz], -1).reshape(GRID, 2 * MODES).T
    fwd = np.stack([np.stack([cf, -sf], -1), np.stack([sf, cf], -1)], 1)
    inv = np.stack(
        [np.stack([cf.T, sf.T], -1), np.stack([-sf.T, cf.T], -1)], 1
    )
    ty = fwd.reshape(COLS, 16, 2, 4, 16, 2)[:, :, :, :, ROW_IN]
    ty = ty.transpose(3, 5, 4, 0, 2, 1).reshape(128, 512)
    tx = fwd.reshape(ROWS, 2, 16, 2, MODES, 2)[:, :, ROW_OUT]
    tx = tx.transpose(5, 4, 0, 1, 3, 2).reshape(128, 512)
    ix = inv.reshape(MODES, 2, ROWS, 2, 16, 2)[:, :, :, :, ROW_IN]
    ix = ix.transpose(2, 3, 5, 4, 1, 0).reshape(512, 128)
    iy = inv.reshape(4, 16, 2, COLS, 16, 2)[:, ROW_OUT]
    iy = iy.transpose(3, 5, 4, 0, 2, 1).reshape(512, 128)
    a = np.where(np.arange(MODES) == 0, 1.0, 2.0)[None, :]
    iz = np.stack([a * cz, -a * sz], -1).reshape(GRID, 2 * MODES)
    return [jnp.asarray(t.astype(np.float32)).astype(BF16) for t in (tz, ty, tx, ix, iy, iz)]


def div_const(v, d):
    return ((v.astype(F32) + 0.5) * (1.0 / d)).astype(jnp.int32)


def pack_kernel(
    row_ref, own_ref, cell_ref, feat_ref, w_ref, corner_ref, mode_hbm,
    send_ref, slot_ref, m1_ref, m2_ref, m3_ref, cnt_ref, head_ref, sem
):
    chip = row_ref[0] // 2
    copies = [
        pltpu.make_async_copy(mode_hbm.at[(chip + 1 + i) % 4], out, sem.at[i])
        for i, out in enumerate((m1_ref, m2_ref, m3_ref))
    ]
    for copy in copies:
        copy.start()
    zero = jnp.zeros((8, 56, NPTS), BF16)

    @pl.loop(0, NBLK // 8)
    def _(i):
        send_ref[pl.ds(i * 8, 8)] = zero
        head_ref[pl.ds(i * 8, 8)] = jnp.zeros((8, 8, NPTS), F32)

    @pl.loop(0, NBLK, unroll=16)
    def _(i):
        cnt_ref[i] = 0

    row = lax.broadcasted_iota(jnp.int32, (4, NPTS), 0)

    @pl.loop(0, NBLK, unroll=8)
    def _(b):
        o = own_ref[b]
        r = cnt_ref[o]
        cnt_ref[o] = r + 1
        r = jnp.minimum(r, 1)
        slot_ref[b] = o * 2 + r
        at = pl.multiple_of(b * NPTS, NPTS)
        v = jnp.broadcast_to(corner_ref[pl.ds(b, 1), :], (4, NPTS))
        vx = div_const(v, 49)
        rest = v - vx * 49
        vy = div_const(rest, 7)
        vz = rest - vy * 7
        head = jnp.where(
            row == 0, vx, jnp.where(row == 1, vy, jnp.where(row == 2, vz, cell_ref[b] + 1))
        )
        send_ref[o, pl.ds(pl.multiple_of(r * 16, 16), 16), :] = feat_ref[:, pl.ds(at, NPTS)]
        send_ref[o, pl.ds(pl.multiple_of(32 + r * 8, 8), 8), :] = w_ref[:, pl.ds(at, NPTS)]
        head_ref[o, pl.ds(r * 4, 4), :] = head.astype(F32)

    @pl.loop(0, NBLK // 8)
    def _(i):
        send_ref[pl.ds(i * 8, 8), 48:56, :] = head_ref[pl.ds(i * 8, 8)].astype(BF16)

    for copy in copies:
        copy.wait()


def pack(row, owner, cell, features, weights, corner, modes):
    smem = pl.BlockSpec(memory_space=pltpu.SMEM)
    vmem = pl.BlockSpec(memory_space=pltpu.VMEM)
    hbm = pl.BlockSpec(memory_space=pl.ANY)
    part = jax.ShapeDtypeStruct((8, CH, CH, 128), BF16)
    return pl.pallas_call(
        pack_kernel,
        out_shape=(
            jax.ShapeDtypeStruct((NBLK, 56, NPTS), BF16),
            jax.ShapeDtypeStruct((NBLK,), jnp.int32),
            part,
            part,
            part,
        ),
        in_specs=[smem, smem, smem, vmem, vmem, vmem, hbm],
        out_specs=(vmem, smem, vmem, vmem, vmem),
        scratch_shapes=[
            pltpu.SMEM((NBLK,), jnp.int32),
            pltpu.VMEM((NBLK, 8, NPTS), F32),
            pltpu.SemaphoreType.DMA((3,)),
        ],
        name="pack",
    )(row, owner, cell, features, weights, corner, modes)


def yz_basis(w, head):
    zi = lax.broadcasted_iota(jnp.int32, (8, NPTS), 0).astype(F32)
    bc = lambda k: jnp.broadcast_to(w[k : k + 1, :], (8, NPTS))
    vy = jnp.broadcast_to(head[1:2, :], (8, NPTS))
    vz = jnp.broadcast_to(head[2:3, :], (8, NPTS))
    m0 = zi == vz
    m1 = zi == vz + 1.0
    zero = jnp.zeros((8, NPTS), F32)
    zc = [
        [
            jnp.where(m0, bc(4 * dx + 2 * dy), jnp.where(m1, bc(4 * dx + 2 * dy + 1), zero))
            for dy in range(2)
        ]
        for dx in range(2)
    ]
    my = [vy == float(y) for y in range(7)]
    halves = []
    for dx in range(2):
        rows = []
        for y in range(8):
            val = zero
            if y > 0:
                val = jnp.where(my[y - 1], zc[dx][1], val)
            if y < 7:
                val = jnp.where(my[y], zc[dx][0], val)
            rows.append(val)
        halves.append(jnp.concatenate(rows, 0).astype(BF16))
    return jnp.concatenate(halves, 1)


def split_lanes(a, b):
    low = lax.broadcasted_iota(jnp.int32, a.shape, a.ndim - 1) < 64
    first = jnp.where(low, a, pltpu.roll(b, 64, a.ndim - 1))
    second = jnp.where(low, pltpu.roll(a, 64, a.ndim - 1), b)
    return first, second


def scatter_kernel(
    recv_hbm, tz_ref, field_hbm, out_hbm, ids_ref,
    recv_ref, g_ref, z_ref, field_ref, out_ref, in_sem, field_sem, out_sem, *, unroll
):
    part = NBLK // 4

    def fetch(k):
        at = pl.ds(k * part, part)
        return pltpu.make_async_copy(recv_hbm.at[at], recv_ref.at[at], in_sem.at[k])

    for k in range(4):
        fetch(k).start()
    zero = jnp.zeros((4, 64, 128), F32)

    @pl.loop(0, 64)
    def _(i):
        g_ref[pl.ds(i * 4, 4)] = zero

    @pl.loop(0, 4)
    def _(k):
        fetch(k).wait()

        @pl.loop(0, part // unroll)
        def _(i):
            for u in range(unroll):
                d = k * part + i * unroll + u
                weights = recv_ref[d, 32:48, :].astype(F32)
                heads = recv_ref[d, 48:56, :].astype(F32)
                for j in range(2):
                    head = heads[4 * j : 4 * j + 4]
                    basis = yz_basis(weights[8 * j : 8 * j + 8], head)
                    feat = recv_ref[d, 16 * j : 16 * j + 16, :].astype(F32)
                    vx = jnp.broadcast_to(head[0:1, :], (8, NPTS))
                    zf = jnp.zeros((8, NPTS), F32)
                    low, high = [], []
                    for ch in range(2):
                        half = feat[ch * 8 : ch * 8 + 8]
                        sel = [jnp.where(vx == float(x), half, 0.0) for x in range(7)]
                        low += sel + [zf]
                        high += [zf] + sel
                    lhs = jnp.concatenate(
                        [
                            jnp.concatenate(low, 0).astype(BF16),
                            jnp.concatenate(high, 0).astype(BF16),
                        ],
                        1,
                    )
                    res = mm(basis, lhs, NT)
                    b = jnp.clip(head[3, 0].astype(jnp.int32) - 1, 0, 255)
                    ids_ref[2 * d + j] = b
                    g_ref[b] = g_ref[b] + res

    tz = tz_ref[...]

    def put_field(q):
        at = pl.ds(q * 8, 8)
        return pltpu.make_async_copy(field_ref.at[at], field_hbm.at[at], field_sem.at[q])

    def put_out(s):
        return pltpu.make_async_copy(out_ref.at[s], out_hbm.at[:, s], out_sem.at[s])

    @pl.loop(0, 8, unroll=2)
    def _(q):
        bx = q // 2
        by = q % 2
        for h in range(4):
            ms = []
            for yl in (2 * h, 2 * h + 1):
                m = g_ref[pl.ds(q * 32, 32), yl * 8 : yl * 8 + 8, :].reshape(GRID, 128)
                m = m.astype(BF16)
                field_ref[q * 8 + yl] = m
                ms.append(m)
            res = mm(tz, jnp.concatenate(ms, 1))
            for e in range(2):
                y = by * 8 + 2 * h + e
                z_ref[bx, pl.ds(y, 128, stride=16), :] = res[:, e * 128 : e * 128 + 128]
        put_field(q).start()

    @pl.loop(0, 16, unroll=4)
    def _(s):
        for kz in range(4):
            for ri in range(2):
                at = pl.multiple_of(s * 128 + kz * 32 + ri * 16, 16)
                for p in range(2):
                    pair = split_lanes(
                        z_ref[2 * p, pl.ds(at, 16), :], z_ref[2 * p + 1, pl.ds(at, 16), :]
                    )
                    for ch in range(2):
                        out_ref[s, 2 * kz + ch, ri, p] = pair[ch].astype(BF16)
        put_out(s).start()

    @pl.loop(0, 8)
    def _(q):
        put_field(q).wait()

    @pl.loop(0, 16)
    def _(s):
        put_out(s).wait()


def scatter(recv, tz):
    smem = pl.BlockSpec(memory_space=pltpu.SMEM)
    vmem = pl.BlockSpec(memory_space=pltpu.VMEM)
    hbm = pl.BlockSpec(memory_space=pl.ANY)
    return pl.pallas_call(
        partial(scatter_kernel, unroll=16),
        out_shape=(
            jax.ShapeDtypeStruct((64, GRID, 128), BF16),
            jax.ShapeDtypeStruct((8, 16, 2, 2, 16, 128), BF16),
            jax.ShapeDtypeStruct((NSLOT,), jnp.int32),
        ),
        in_specs=[hbm, vmem],
        out_specs=(hbm, hbm, smem),
        scratch_shapes=[
            pltpu.VMEM((NBLK, 56, NPTS), BF16),
            pltpu.VMEM((256, 64, 128), F32),
            pltpu.VMEM((4, 2048, 128), F32),
            pltpu.VMEM((64, GRID, 128), BF16),
            pltpu.VMEM((16, 8, 2, 2, 16, 128), BF16),
            pltpu.SemaphoreType.DMA((4,)),
            pltpu.SemaphoreType.DMA((8,)),
            pltpu.SemaphoreType.DMA((16,)),
        ],
        name="scatter_z",
    )(recv, tz)


def group_transpose(x):
    n = x.shape[0]
    low, high = x[:, 0:8], x[:, 8:16]
    even = (lax.broadcasted_iota(jnp.int32, low.shape, 2) // 8) % 2 == 0
    first = jnp.where(even, low, pltpu.roll(high, 8, 2))
    second = jnp.where(even, pltpu.roll(low, 120, 2), high)
    x = jnp.concatenate([first, second], 0)
    group = lax.broadcasted_iota(jnp.int32, x.shape, 2) // 16
    x = pltpu.roll(x, 0, 2, stride=16, stride_axis=1)
    for k in range(3):
        d = 1 << k
        x = jnp.where((group // d) % 2 == 1, pltpu.roll(x, 8 - d, 1), x)
    x = pltpu.roll(x, 0, 2, stride=16, stride_axis=1)
    return jnp.concatenate([x[:n], x[n:]], 1)


def yx_kernel(row_ref, in_hbm, ty_ref, tx_ref, keep_ref, send_ref, in_ref, v_ref, sem):
    def get(r):
        at = pl.ds(r * COLS, COLS)
        return pltpu.make_async_copy(in_hbm.at[at], in_ref.at[at], sem.at[r])

    for r in range(8):
        get(r).start()

    @pl.loop(0, 8, unroll=2)
    def _(r):
        get(r).wait()
        at = pl.ds(r * COLS, COLS)
        rhs = jnp.concatenate([in_ref[at, :, p].reshape(512, 128) for p in range(2)], 1)
        res = mm(ty_ref[...], rhs)
        for p in range(2):
            tiles = group_transpose(res[:, p * 128 : p * 128 + 128].reshape(8, 16, 128))
            tiles = tiles.reshape(4, 32, 128).astype(BF16)
            to = pl.multiple_of(r * 64 + p * 32, 32)
            for g in range(4):
                v_ref[g, pl.ds(to, 32), :] = tiles[g]

    first = row_ref[0] % 2 == 0
    for g in range(4):
        spec = mm(tx_ref[...], v_ref[g]).T
        keep, send = choose(first, spec[0:64], spec[64:128])
        keep_ref[g] = keep.astype(BF16)
        send_ref[g] = send.astype(BF16)


def choose(first, a, b):
    return jnp.where(first, a, b), jnp.where(first, b, a)


def yx_forward(row, zs, ty, tx):
    smem = pl.BlockSpec(memory_space=pltpu.SMEM)
    vmem = pl.BlockSpec(memory_space=pltpu.VMEM)
    hbm = pl.BlockSpec(memory_space=pl.ANY)
    return pl.pallas_call(
        yx_kernel,
        out_shape=(jax.ShapeDtypeStruct((4, 64, 128), BF16),) * 2,
        in_specs=[smem, hbm, vmem, vmem],
        out_specs=(vmem, vmem),
        scratch_shapes=[
            pltpu.VMEM((128, 2, 2, 16, 128), BF16),
            pltpu.VMEM((4, 512, 128), BF16),
            pltpu.SemaphoreType.DMA((8,)),
        ],
        name="yx_forward",
    )(row, zs, ty, tx)


def mix_kernel(
    row_ref, own_ref, got_ref, mode_hbm, m1_hbm, m2_hbm, m3_hbm, keep_ref, send_ref, w_ref, sem
):
    chip = row_ref[0] // 2
    first = row_ref[0] % 2 == 0
    copies = [
        pltpu.make_async_copy(src, w_ref.at[d], sem.at[d])
        for d, src in enumerate((mode_hbm.at[chip], m1_hbm, m2_hbm, m3_hbm))
    ]
    for copy in copies:
        copy.start()
    lane = lax.broadcasted_iota(jnp.int32, (16, 128), 1)

    for d in range(4):
        copies[d].wait()
        j = (chip + 4 - d) % 4
        spec = choose(first, own_ref[j].astype(F32), got_ref[j].astype(F32))
        swapped = [pltpu.roll(x, 64, 1) for x in spec]
        halves = [[], []]
        for ky in range(8):
            a1 = jnp.zeros((16, 128), F32)
            a2 = jnp.zeros((16, 128), F32)
            for c in range(CH):
                w = w_ref[d, ky, c].astype(F32)
                at = ky * 8 + c % 8
                a1 = a1 + spec[c // 8][at : at + 1, :] * w
                a2 = a2 + swapped[c // 8][at : at + 1, :] * w
            res = jnp.where(lane < 64, a1 - pltpu.roll(a1, 64, 1), a2 + pltpu.roll(a2, 64, 1))
            for h in range(2):
                halves[h].append(res[h * 8 : h * 8 + 8])
        keep, send = choose(first, *[jnp.concatenate(half, 0) for half in halves])
        keep_ref[j] = keep.astype(BF16)
        send_ref[j] = send.astype(BF16)


def mix(row, own, got, modes, parts):
    smem = pl.BlockSpec(memory_space=pltpu.SMEM)
    vmem = pl.BlockSpec(memory_space=pltpu.VMEM)
    hbm = pl.BlockSpec(memory_space=pl.ANY)
    return pl.pallas_call(
        mix_kernel,
        out_shape=(jax.ShapeDtypeStruct((4, 64, 128), BF16),) * 2,
        in_specs=[smem, vmem, vmem, hbm, hbm, hbm, hbm],
        out_specs=(vmem, vmem),
        scratch_shapes=[
            pltpu.VMEM((4, 8, CH, CH, 128), BF16),
            pltpu.SemaphoreType.DMA((4,)),
        ],
        name="mix",
    )(row, own, got, modes, *parts)


def xy_kernel(row_ref, own_ref, got_ref, ix_ref, iy_ref, out_hbm, u_ref, out_ref, sem):
    def put(r):
        at = pl.ds(r * COLS, COLS)
        return pltpu.make_async_copy(out_ref.at[at], out_hbm.at[at], sem.at[r])

    @pl.loop(0, 4, unroll=2)
    def _(g):
        pair = choose(row_ref[0] % 2 == 0, own_ref[g].astype(F32), got_ref[g].astype(F32))
        rhs = jnp.concatenate(pair, 0).astype(BF16)
        xi = group_transpose(mm(ix_ref[...], rhs, NT).reshape(32, 16, 128))
        u_ref[g] = xi.astype(BF16)

    @pl.loop(0, 8, unroll=2)
    def _(r):
        rhs = jnp.concatenate(
            [u_ref[:, pl.ds(r * 4 + p * 2, 2)].reshape(128, 128) for p in range(2)], 1
        )
        res = mm(iy_ref[...], rhs).astype(BF16)
        for s in range(16):
            for ri in range(2):
                at = s * 32 + ri * 16
                for p in range(2):
                    out_ref[r * COLS + s, ri, p] = res[at : at + 16, p * 128 : p * 128 + 128]
        put(r).start()

    for r in range(8):
        put(r).wait()


def xy_inverse(row, own, got, ix, iy):
    smem = pl.BlockSpec(memory_space=pltpu.SMEM)
    vmem = pl.BlockSpec(memory_space=pltpu.VMEM)
    hbm = pl.BlockSpec(memory_space=pl.ANY)
    return pl.pallas_call(
        xy_kernel,
        out_shape=jax.ShapeDtypeStruct((128, 2, 2, 16, 128), BF16),
        in_specs=[smem, vmem, vmem, vmem, vmem],
        out_specs=hbm,
        scratch_shapes=[
            pltpu.VMEM((4, 32, 16, 128), BF16),
            pltpu.VMEM((128, 2, 2, 16, 128), BF16),
            pltpu.SemaphoreType.DMA((8,)),
        ],
        name="xy_inverse",
    )(row, own, got, ix, iy)


def gelu(x):
    x = x.astype(BF16)
    c = math.sqrt(2.0 / math.pi)
    t = jnp.tanh(x * (jnp.asarray(c, BF16) + jnp.asarray(c * 0.044715, BF16) * (x * x)))
    h = x * jnp.asarray(0.5, BF16)
    return h + h * t


def expand_weights(in_ref, skip_ref, out_ref, w1_ref, w2_ref):
    iota = lambda shape, d: lax.broadcasted_iota(jnp.int32, shape, d)
    hot = lambda cond: jnp.where(cond, 1.0, 0.0).astype(BF16)
    rep = hot(iota((HID, 512), 0) == iota((HID, 512), 1) % HID)
    row = iota((128, CH), 0)
    chan = hot((row // 64) * 8 + row % 8 == iota((128, CH), 1))
    keep = (iota((128, 512), 0) // 8) % 8 == iota((128, 512), 1) // HID
    first = in_ref[...]
    both = mm(skip_ref[...], first, TN).astype(BF16)
    for e, w in enumerate((first, both)):
        full = mm(chan, mm(w, rep).astype(BF16))
        w1_ref[e * 128 : e * 128 + 128, :] = jnp.where(keep, full, 0.0).astype(BF16)
    rows = hot(iota((512, HID), 0) % HID == iota((512, HID), 1))
    cols = hot(iota((CH, 128), 1) % CH == iota((CH, 128), 0))
    full = mm(mm(rows, out_ref[...], NT).astype(BF16), cols)
    keep = iota((512, 128), 0) // HID == iota((512, 128), 1) // CH
    w2_ref[...] = jnp.where(keep, full, 0.0).astype(BF16)


def final_kernel(
    ids_ref, yi_hbm, field_hbm, recv_hbm, iz_ref, in_ref, skip_ref, bias_ref, mout_ref, out_hbm,
    yi_ref, field_ref, tail_ref, out_ref, y_ref, xa_ref, xb_ref, l_ref, w1_ref, w2_ref, b1_ref,
    yi_sem, field_sem, tail_sem, out_sem, *, ny, unroll
):
    def get_yi(r):
        at = pl.ds(r * COLS, COLS)
        return pltpu.make_async_copy(yi_hbm.at[at], yi_ref.at[at], yi_sem.at[r])

    def put_out(i):
        at = pl.ds(i * 2 * unroll, 2 * unroll)
        return pltpu.make_async_copy(out_ref.at[at], out_hbm.at[at], out_sem.at[i])

    get_field = pltpu.make_async_copy(field_hbm, field_ref, field_sem)
    get_tail = pltpu.make_async_copy(recv_hbm.at[:, 32:56], tail_ref, tail_sem)

    @pl.loop(0, 8)
    def _(r):
        get_yi(r).start()

    get_field.start()
    get_tail.start()
    expand_weights(in_ref, skip_ref, mout_ref, w1_ref, w2_ref)
    b1_ref[...] = jnp.concatenate([bias_ref[...]] * 8, 1)

    @pl.loop(0, 4)
    def _(kz):
        get_yi(2 * kz).wait()
        get_yi(2 * kz + 1).wait()

        @pl.loop(0, 16, unroll=4)
        def _(s):
            for ri in range(2):
                at = pl.multiple_of(s * 128 + kz * 32 + ri * 16, 16)
                for p in range(2):
                    pair = split_lanes(
                        yi_ref[kz * 32 + s, ri, p].astype(F32),
                        yi_ref[kz * 32 + 16 + s, ri, p].astype(F32),
                    )
                    for e in range(2):
                        y_ref[2 * p + e, pl.ds(at, 16), :] = pair[e]

    def stage(i, x_ref):
        base = i * ny
        bx = base // 16
        for p in range(ny // 2):
            y = (base + 2 * p) % 16
            rhs = jnp.concatenate(
                [y_ref[bx, pl.ds(y + e, 128, stride=16), :] for e in range(2)], 1
            ).astype(BF16)
            res = mm(iz_ref[...], rhs).astype(BF16)
            for e in range(2):
                at = (2 * p + e) * GRID
                x_ref[at : at + GRID, 0:128] = res[:, e * 128 : e * 128 + 128]
                x_ref[at : at + GRID, 128:256] = field_ref[base + 2 * p + e]

    def layer(i, x_ref):
        h = gelu(mm(x_ref[...], w1_ref[...]) + b1_ref[...])
        o = mm(h, w2_ref[...]).astype(BF16).astype(F32)
        l_ref[pl.ds(i * ny, ny)] = o.reshape(ny, GRID, 128)

    steps = 64 // ny
    get_field.wait()
    stage(0, xa_ref)

    @pl.loop(0, steps // 2)
    def _(i):
        stage(2 * i + 1, xb_ref)
        layer(2 * i, xa_ref)
        stage(jnp.minimum(2 * i + 2, steps - 1), xa_ref)
        layer(2 * i + 1, xb_ref)

    get_tail.wait()

    @pl.loop(0, NBLK // unroll)
    def _(i):
        for u in range(unroll):
            d = i * unroll + u
            weights = tail_ref[d, 0:16, :].astype(F32)
            heads = tail_ref[d, 16:24, :].astype(F32)
            for j in range(2):
                head = heads[4 * j : 4 * j + 4]
                basis = yz_basis(weights[8 * j : 8 * j + 8], head)
                b = ids_ref[2 * d + j]
                q = b // 32
                at = pl.multiple_of((b % 32) * 8, 8)
                cells = l_ref[pl.ds(q * 8, 8), pl.ds(at, 8), :].reshape(64, 128).astype(BF16)
                res = mm(cells, basis, TN)
                vx = jnp.broadcast_to(head[0:1, :], (16, NPTS))
                val = jnp.zeros((16, NPTS), F32)
                for x in range(7):
                    got = (
                        res[x * 16 : x * 16 + 16, 0:128]
                        + res[x * 16 + 16 : x * 16 + 32, 128:256]
                    )
                    val = jnp.where(vx == float(x), got, val)
                out_ref[2 * d + j] = val.astype(BF16)
        put_out(i).start()

    @pl.loop(0, NBLK // unroll)
    def _(i):
        put_out(i).wait()


def final(ids, yi, field, recv, iz, first, skip, bias, mout):
    smem = pl.BlockSpec(memory_space=pltpu.SMEM)
    vmem = pl.BlockSpec(memory_space=pltpu.VMEM)
    hbm = pl.BlockSpec(memory_space=pl.ANY)
    ny, unroll = 8, 16
    return pl.pallas_call(
        partial(final_kernel, ny=ny, unroll=unroll),
        out_shape=jax.ShapeDtypeStruct((NSLOT, 16, NPTS), BF16),
        in_specs=[smem, hbm, hbm, hbm, vmem, vmem, vmem, vmem, vmem],
        out_specs=hbm,
        scratch_shapes=[
            pltpu.VMEM((128, 2, 2, 16, 128), BF16),
            pltpu.VMEM((64, GRID, 128), BF16),
            pltpu.VMEM((NBLK, 24, NPTS), BF16),
            pltpu.VMEM((NSLOT, 16, NPTS), BF16),
            pltpu.VMEM((4, 2048, 128), F32),
            pltpu.VMEM((ny * GRID, 256), BF16),
            pltpu.VMEM((ny * GRID, 256), BF16),
            pltpu.VMEM((64, GRID, 128), F32),
            pltpu.VMEM((256, 512), BF16),
            pltpu.VMEM((512, 128), BF16),
            pltpu.VMEM((1, 512), F32),
            pltpu.SemaphoreType.DMA((8,)),
            pltpu.SemaphoreType.DMA,
            pltpu.SemaphoreType.DMA,
            pltpu.SemaphoreType.DMA((NBLK // unroll,)),
        ],
        name="mlp_gather",
    )(ids, yi, field, recv, iz, first, skip, bias, mout)


def unpack_kernel(slot_ref, in_ref, out_ref):
    @pl.loop(0, NBLK, unroll=8)
    def _(b):
        at = pl.multiple_of(b * NPTS, NPTS)
        out_ref[:, pl.ds(at, NPTS)] = in_ref[slot_ref[b]]


def unpack(slots, vals):
    smem = pl.BlockSpec(memory_space=pltpu.SMEM)
    vmem = pl.BlockSpec(memory_space=pltpu.VMEM)
    return pl.pallas_call(
        unpack_kernel,
        out_shape=jax.ShapeDtypeStruct((CH, NBLK * NPTS), BF16),
        in_specs=[smem, vmem],
        out_specs=vmem,
        name="unpack",
    )(slots, vals)


def a2a(x, axes):
    return lax.all_to_all(x, axes, split_axis=0, concat_axis=0, tiled=True)


def partner(x):
    return lax.ppermute(x, "row", [(i, i ^ 1) for i in range(ROWS)])


def body(
    features,
    point_weights,
    point_corner,
    block_owner,
    block_cell,
    spec_weight,
    skip_weight,
    mlp_in,
    mlp_bias,
    mlp_out,
):
    tz, ty, tx, ix, iy, iz = tables()
    owner = block_owner.reshape(NBLK)
    row = lax.axis_index("row").astype(jnp.int32)[None]
    corner = point_corner.reshape(NBLK, NPTS)
    send, slots, *parts = pack(
        row, owner, block_cell, features, point_weights, corner, spec_weight
    )
    parts = [
        lax.ppermute(part, "row", [(i, (i + 2 * d) % ROWS) for i in range(ROWS)])
        for d, part in zip((1, 2, 3), parts)
    ]
    recv = a2a(send, ("row", "col"))
    field, zs, ids = scatter(recv, tz)
    zs = a2a(zs.reshape(128, 2, 2, 16, 128), ("row", "col"))
    keep, send = yx_forward(row, zs, ty, tx)
    keep, send = mix(row, keep, partner(send), spec_weight, parts)
    yi = a2a(xy_inverse(row, keep, partner(send), ix, iy), ("row", "col"))
    vals = final(
        ids, yi, field, recv, iz, mlp_in.T, skip_weight, mlp_bias.reshape(1, HID), mlp_out
    )
    return unpack(slots, a2a(vals, ("row", "col")))


def solution(mesh):
    return jax.shard_map(
        body,
        mesh=mesh,
        in_specs=(
            P(None, ("row", "col")),
            P(None, ("row", "col")),
            P(("row", "col")),
            P(("row", "col"), None),
            P(("row", "col")),
            P("col", "row", None, None, None),
            P(),
            P(),
            P(),
            P(),
        ),
        out_specs=P(None, ("row", "col")),
        check_vma=False,
    )
```

```python
import math
from functools import partial

import jax
import jax.numpy as jnp
import numpy as np
from jax import lax
from jax.experimental import pallas as pl
from jax.experimental.pallas import tpu as pltpu
from jax.sharding import PartitionSpec as P

GRID = 256
MODES = 64
NPTS = 128
NBLK = 128
NSLOT = 256
ROWS = 8
COLS = 16
CH = 16
HID = 64
F32 = jnp.float32
BF16 = jnp.bfloat16
NN = (((1,), (0,)), ((), ()))
NT = (((1,), (1,)), ((), ()))
TN = (((0,), (0,)), ((), ()))


def near(x):
    return pltpu.with_memory_space_constraint(x, pltpu.VMEM)


def grant(mib):
    return pltpu.CompilerParams(vmem_limit_bytes=mib << 20)


def mm(a, b, dims=NN):
    return lax.dot_general(a, b, dims, preferred_element_type=F32)


ROW_IN = np.array([2 * lo + hi for hi in range(2) for lo in range(8)])
ROW_OUT = np.array([2 * ((-t) % 8) + v for v in range(2) for t in range(8)])


def _freqs():
    j = np.arange(MODES)
    return np.where(j < MODES // 2, j, GRID - MODES + j)


def _trig(freq):
    turns = (np.arange(GRID)[:, None] * freq[None, :]) % GRID
    theta = (2.0 * math.pi / GRID) * turns
    f = 1.0 / math.sqrt(GRID)
    return np.cos(theta) * f, np.sin(theta) * f


def tables():
    cz, sz = _trig(np.arange(MODES))
    cf, sf = _trig(_freqs())
    tz = np.stack([cz, -sz], -1).reshape(GRID, 2 * MODES).T
    fwd = np.stack([np.stack([cf, -sf], -1), np.stack([sf, cf], -1)], 1)
    inv = np.stack(
        [np.stack([cf.T, sf.T], -1), np.stack([-sf.T, cf.T], -1)], 1
    )
    ty = fwd.reshape(COLS, 16, 2, 4, 16, 2)[:, :, :, :, ROW_IN]
    ty = ty.transpose(3, 5, 4, 0, 2, 1).reshape(128, 512)
    tx = fwd.reshape(ROWS, 2, 16, 2, MODES, 2)[:, :, ROW_OUT]
    tx = tx.transpose(5, 4, 0, 1, 3, 2).reshape(128, 512)
    ix = inv.reshape(MODES, 2, ROWS, 2, 16, 2)[:, :, :, :, ROW_IN]
    ix = ix.transpose(2, 3, 5, 4, 1, 0).reshape(512, 128)
    iy = inv.reshape(4, 16, 2, COLS, 16, 2)[:, ROW_OUT]
    iy = iy.transpose(3, 5, 4, 0, 2, 1).reshape(512, 128)
    a = np.where(np.arange(MODES) == 0, 1.0, 2.0)[None, :]
    iz = np.stack([a * cz, -a * sz], -1).reshape(GRID, 2 * MODES)
    return [jnp.asarray(t.astype(np.float32)).astype(BF16) for t in (tz, ty, tx, ix, iy, iz)]


def div_const(v, d):
    return ((v.astype(F32) + 0.5) * (1.0 / d)).astype(jnp.int32)


def pack_kernel(
    row_ref, own_ref, cell_ref, feat_ref, w_ref, corner_ref, mode_hbm,
    send_ref, slot_ref, m1_ref, m2_ref, m3_ref, cnt_ref, head_ref, sem
):
    chip = row_ref[0] // 2
    copies = [
        pltpu.make_async_copy(mode_hbm.at[(chip + 1 + i) % 4], out, sem.at[i])
        for i, out in enumerate((m1_ref, m2_ref, m3_ref))
    ]
    for copy in copies:
        copy.start()
    zero = jnp.zeros((8, 56, NPTS), BF16)

    @pl.loop(0, NBLK // 8)
    def _(i):
        send_ref[pl.ds(i * 8, 8)] = zero
        head_ref[pl.ds(i * 8, 8)] = jnp.zeros((8, 8, NPTS), F32)

    @pl.loop(0, NBLK, unroll=16)
    def _(i):
        cnt_ref[i] = 0

    row = lax.broadcasted_iota(jnp.int32, (4, NPTS), 0)

    @pl.loop(0, NBLK, unroll=8)
    def _(b):
        o = own_ref[b]
        r = cnt_ref[o]
        cnt_ref[o] = r + 1
        r = jnp.minimum(r, 1)
        slot_ref[b] = o * 2 + r
        at = pl.multiple_of(b * NPTS, NPTS)
        v = jnp.broadcast_to(corner_ref[pl.ds(b, 1), :], (4, NPTS))
        vx = div_const(v, 49)
        rest = v - vx * 49
        vy = div_const(rest, 7)
        vz = rest - vy * 7
        head = jnp.where(
            row == 0, vx, jnp.where(row == 1, vy, jnp.where(row == 2, vz, cell_ref[b] + 1))
        )
        send_ref[o, pl.ds(pl.multiple_of(r * 16, 16), 16), :] = feat_ref[:, pl.ds(at, NPTS)]
        send_ref[o, pl.ds(pl.multiple_of(32 + r * 8, 8), 8), :] = w_ref[:, pl.ds(at, NPTS)]
        head_ref[o, pl.ds(r * 4, 4), :] = head.astype(F32)

    @pl.loop(0, NBLK // 8)
    def _(i):
        send_ref[pl.ds(i * 8, 8), 48:56, :] = head_ref[pl.ds(i * 8, 8)].astype(BF16)

    for copy in copies:
        copy.wait()


def pack(row, owner, cell, features, weights, corner, modes):
    smem = pl.BlockSpec(memory_space=pltpu.SMEM)
    vmem = pl.BlockSpec(memory_space=pltpu.VMEM)
    hbm = pl.BlockSpec(memory_space=pltpu.HBM)
    part = pltpu.HBM((8, CH, CH, 128), BF16)
    return pl.pallas_call(
        pack_kernel,
        out_shape=(
            pltpu.HBM((NBLK, 56, NPTS), BF16),
            jax.ShapeDtypeStruct((NBLK,), jnp.int32),
            part,
            part,
            part,
        ),
        in_specs=[smem, smem, smem, vmem, vmem, vmem, hbm],
        out_specs=(vmem, smem, vmem, vmem, vmem),
        scratch_shapes=[
            pltpu.SMEM((NBLK,), jnp.int32),
            pltpu.VMEM((NBLK, 8, NPTS), F32),
            pltpu.SemaphoreType.DMA((3,)),
        ],
        compiler_params=grant(16),
        name="pack",
    )(row, owner, cell, features, weights, corner, modes)


def yz_basis(w, head):
    zi = lax.broadcasted_iota(jnp.int32, (8, NPTS), 0).astype(F32)
    bc = lambda k: jnp.broadcast_to(w[k : k + 1, :], (8, NPTS))
    vy = jnp.broadcast_to(head[1:2, :], (8, NPTS))
    vz = jnp.broadcast_to(head[2:3, :], (8, NPTS))
    m0 = zi == vz
    m1 = zi == vz + 1.0
    zero = jnp.zeros((8, NPTS), F32)
    zc = [
        [
            jnp.where(m0, bc(4 * dx + 2 * dy), jnp.where(m1, bc(4 * dx + 2 * dy + 1), zero))
            for dy in range(2)
        ]
        for dx in range(2)
    ]
    my = [vy == float(y) for y in range(7)]
    halves = []
    for dx in range(2):
        rows = []
        for y in range(8):
            val = zero
            if y > 0:
                val = jnp.where(my[y - 1], zc[dx][1], val)
            if y < 7:
                val = jnp.where(my[y], zc[dx][0], val)
            rows.append(val)
        halves.append(jnp.concatenate(rows, 0).astype(BF16))
    return jnp.concatenate(halves, 1)


def split_lanes(a, b):
    low = lax.broadcasted_iota(jnp.int32, a.shape, a.ndim - 1) < 64
    first = jnp.where(low, a, pltpu.roll(b, 64, a.ndim - 1))
    second = jnp.where(low, pltpu.roll(a, 64, a.ndim - 1), b)
    return first, second


def scatter_kernel(
    recv_ref, tz_ref, field_ref, out_ref, ids_ref, g_ref, z_ref, *, unroll
):
    zero = jnp.zeros((4, 64, 128), F32)

    @pl.loop(0, 64)
    def _(i):
        g_ref[pl.ds(i * 4, 4)] = zero

    @pl.loop(0, NBLK // unroll)
    def _(i):
        for u in range(unroll):
            d = i * unroll + u
            weights = recv_ref[d, 32:48, :].astype(F32)
            heads = recv_ref[d, 48:56, :].astype(F32)
            for j in range(2):
                head = heads[4 * j : 4 * j + 4]
                basis = yz_basis(weights[8 * j : 8 * j + 8], head)
                feat = recv_ref[d, 16 * j : 16 * j + 16, :].astype(F32)
                vx = jnp.broadcast_to(head[0:1, :], (8, NPTS))
                zf = jnp.zeros((8, NPTS), F32)
                low, high = [], []
                for ch in range(2):
                    half = feat[ch * 8 : ch * 8 + 8]
                    sel = [jnp.where(vx == float(x), half, 0.0) for x in range(7)]
                    low += sel + [zf]
                    high += [zf] + sel
                lhs = jnp.concatenate(
                    [
                        jnp.concatenate(low, 0).astype(BF16),
                        jnp.concatenate(high, 0).astype(BF16),
                    ],
                    1,
                )
                res = mm(basis, lhs, NT)
                b = jnp.clip(head[3, 0].astype(jnp.int32) - 1, 0, 255)
                ids_ref[2 * d + j] = b
                g_ref[b] = g_ref[b] + res

    tz = tz_ref[...]

    @pl.loop(0, 8, unroll=2)
    def _(q):
        bx = q // 2
        by = q % 2
        for h in range(4):
            ms = []
            for yl in (2 * h, 2 * h + 1):
                m = g_ref[pl.ds(q * 32, 32), yl * 8 : yl * 8 + 8, :].reshape(GRID, 128)
                m = m.astype(BF16)
                field_ref[q * 8 + yl] = m
                ms.append(m)
            res = mm(tz, jnp.concatenate(ms, 1))
            for e in range(2):
                y = by * 8 + 2 * h + e
                z_ref[bx, pl.ds(y, 128, stride=16), :] = res[:, e * 128 : e * 128 + 128]

    @pl.loop(0, 16, unroll=4)
    def _(s):
        for kz in range(4):
            for ri in range(2):
                at = pl.multiple_of(s * 128 + kz * 32 + ri * 16, 16)
                for p in range(2):
                    pair = split_lanes(
                        z_ref[2 * p, pl.ds(at, 16), :], z_ref[2 * p + 1, pl.ds(at, 16), :]
                    )
                    for ch in range(2):
                        out_ref[2 * kz + ch, s, ri, p] = pair[ch].astype(BF16)


def scatter(recv, tz):
    smem = pl.BlockSpec(memory_space=pltpu.SMEM)
    vmem = pl.BlockSpec(memory_space=pltpu.VMEM)
    return pl.pallas_call(
        partial(scatter_kernel, unroll=16),
        out_shape=(
            pltpu.VMEM((64, GRID, 128), BF16),
            pltpu.VMEM((8, 16, 2, 2, 16, 128), BF16),
            jax.ShapeDtypeStruct((NSLOT,), jnp.int32),
        ),
        in_specs=[vmem, vmem],
        out_specs=(vmem, vmem, smem),
        scratch_shapes=[
            pltpu.VMEM((256, 64, 128), F32),
            pltpu.VMEM((4, 2048, 128), F32),
        ],
        compiler_params=grant(24),
        name="scatter_z",
    )(recv, tz)


def group_transpose(x):
    n = x.shape[0]
    low, high = x[:, 0:8], x[:, 8:16]
    even = (lax.broadcasted_iota(jnp.int32, low.shape, 2) // 8) % 2 == 0
    first = jnp.where(even, low, pltpu.roll(high, 8, 2))
    second = jnp.where(even, pltpu.roll(low, 120, 2), high)
    x = jnp.concatenate([first, second], 0)
    group = lax.broadcasted_iota(jnp.int32, x.shape, 2) // 16
    x = pltpu.roll(x, 0, 2, stride=16, stride_axis=1)
    for k in range(3):
        d = 1 << k
        x = jnp.where((group // d) % 2 == 1, pltpu.roll(x, 8 - d, 1), x)
    x = pltpu.roll(x, 0, 2, stride=16, stride_axis=1)
    return jnp.concatenate([x[:n], x[n:]], 1)


def yx_kernel(row_ref, in_ref, ty_ref, tx_ref, keep_ref, send_ref, v_ref):
    @pl.loop(0, 8, unroll=2)
    def _(r):
        at = pl.ds(r * COLS, COLS)
        rhs = jnp.concatenate([in_ref[at, :, p].reshape(512, 128) for p in range(2)], 1)
        res = mm(ty_ref[...], rhs)
        for p in range(2):
            tiles = group_transpose(res[:, p * 128 : p * 128 + 128].reshape(8, 16, 128))
            tiles = tiles.reshape(4, 32, 128).astype(BF16)
            to = pl.multiple_of(r * 64 + p * 32, 32)
            for g in range(4):
                v_ref[g, pl.ds(to, 32), :] = tiles[g]

    first = row_ref[0] % 2 == 0
    for g in range(4):
        spec = mm(tx_ref[...], v_ref[g]).T
        keep, send = choose(first, spec[0:64], spec[64:128])
        keep_ref[g] = keep.astype(BF16)
        send_ref[g] = send.astype(BF16)


def choose(first, a, b):
    return jnp.where(first, a, b), jnp.where(first, b, a)


def yx_forward(row, zs, ty, tx):
    smem = pl.BlockSpec(memory_space=pltpu.SMEM)
    vmem = pl.BlockSpec(memory_space=pltpu.VMEM)
    return pl.pallas_call(
        yx_kernel,
        out_shape=(pltpu.VMEM((4, 64, 128), BF16),) * 2,
        in_specs=[smem, vmem, vmem, vmem],
        out_specs=(vmem, vmem),
        scratch_shapes=[
            pltpu.VMEM((4, 512, 128), BF16),
        ],
        compiler_params=grant(16),
        name="yx_forward",
    )(row, zs, ty, tx)


def mix_kernel(
    row_ref, own_ref, got_ref, mode_hbm, m1_ref, m2_ref, m3_ref, keep_ref, send_ref, m0_ref, sem
):
    chip = row_ref[0] // 2
    first = row_ref[0] % 2 == 0
    copy = pltpu.make_async_copy(mode_hbm.at[chip], m0_ref, sem)
    copy.start()
    lane = lax.broadcasted_iota(jnp.int32, (16, 128), 1)

    for d, w_ref in ((1, m1_ref), (2, m2_ref), (3, m3_ref), (0, m0_ref)):
        if d == 0:
            copy.wait()
        j = (chip + 4 - d) % 4
        spec = choose(first, own_ref[j].astype(F32), got_ref[j].astype(F32))
        swapped = [pltpu.roll(x, 64, 1) for x in spec]
        halves = [[], []]
        for ky in range(8):
            a1 = jnp.zeros((16, 128), F32)
            a2 = jnp.zeros((16, 128), F32)
            for c in range(CH):
                w = w_ref[ky, c].astype(F32)
                at = ky * 8 + c % 8
                a1 = a1 + spec[c // 8][at : at + 1, :] * w
                a2 = a2 + swapped[c // 8][at : at + 1, :] * w
            res = jnp.where(lane < 64, a1 - pltpu.roll(a1, 64, 1), a2 + pltpu.roll(a2, 64, 1))
            for h in range(2):
                halves[h].append(res[h * 8 : h * 8 + 8])
        keep, send = choose(first, *[jnp.concatenate(half, 0) for half in halves])
        keep_ref[j] = keep.astype(BF16)
        send_ref[j] = send.astype(BF16)


def mix(row, own, got, modes, parts):
    smem = pl.BlockSpec(memory_space=pltpu.SMEM)
    vmem = pl.BlockSpec(memory_space=pltpu.VMEM)
    hbm = pl.BlockSpec(memory_space=pltpu.HBM)
    return pl.pallas_call(
        mix_kernel,
        out_shape=(pltpu.VMEM((4, 64, 128), BF16),) * 2,
        in_specs=[smem, vmem, vmem, hbm, vmem, vmem, vmem],
        out_specs=(vmem, vmem),
        scratch_shapes=[
            pltpu.VMEM((8, CH, CH, 128), BF16),
            pltpu.SemaphoreType.DMA,
        ],
        compiler_params=grant(16),
        name="mix",
    )(row, own, got, modes, *parts)


def xy_kernel(row_ref, own_ref, got_ref, ix_ref, iy_ref, out_ref, u_ref):
    @pl.loop(0, 4, unroll=2)
    def _(g):
        pair = choose(row_ref[0] % 2 == 0, own_ref[g].astype(F32), got_ref[g].astype(F32))
        rhs = jnp.concatenate(pair, 0).astype(BF16)
        xi = group_transpose(mm(ix_ref[...], rhs, NT).reshape(32, 16, 128))
        u_ref[g] = xi.astype(BF16)

    @pl.loop(0, 8, unroll=2)
    def _(r):
        rhs = jnp.concatenate(
            [u_ref[:, pl.ds(r * 4 + p * 2, 2)].reshape(128, 128) for p in range(2)], 1
        )
        res = mm(iy_ref[...], rhs).astype(BF16)
        for s in range(16):
            for ri in range(2):
                at = s * 32 + ri * 16
                for p in range(2):
                    out_ref[r * COLS + s, ri, p] = res[at : at + 16, p * 128 : p * 128 + 128]


def xy_inverse(row, own, got, ix, iy):
    smem = pl.BlockSpec(memory_space=pltpu.SMEM)
    vmem = pl.BlockSpec(memory_space=pltpu.VMEM)
    return pl.pallas_call(
        xy_kernel,
        out_shape=pltpu.VMEM((128, 2, 2, 16, 128), BF16),
        in_specs=[smem, vmem, vmem, vmem, vmem],
        out_specs=vmem,
        scratch_shapes=[
            pltpu.VMEM((4, 32, 16, 128), BF16),
        ],
        compiler_params=grant(16),
        name="xy_inverse",
    )(row, own, got, ix, iy)


def gelu(x):
    x = x.astype(BF16)
    c = math.sqrt(2.0 / math.pi)
    t = jnp.tanh(x * (jnp.asarray(c, BF16) + jnp.asarray(c * 0.044715, BF16) * (x * x)))
    h = x * jnp.asarray(0.5, BF16)
    return h + h * t


def expand_weights(in_ref, skip_ref, out_ref, w1_ref, w2_ref):
    iota = lambda shape, d: lax.broadcasted_iota(jnp.int32, shape, d)
    hot = lambda cond: jnp.where(cond, 1.0, 0.0).astype(BF16)
    rep = hot(iota((HID, 512), 0) == iota((HID, 512), 1) % HID)
    row = iota((128, CH), 0)
    chan = hot((row // 64) * 8 + row % 8 == iota((128, CH), 1))
    keep = (iota((128, 512), 0) // 8) % 8 == iota((128, 512), 1) // HID
    first = in_ref[...]
    both = mm(skip_ref[...], first, TN).astype(BF16)
    for e, w in enumerate((first, both)):
        full = mm(chan, mm(w, rep).astype(BF16))
        w1_ref[e * 128 : e * 128 + 128, :] = jnp.where(keep, full, 0.0).astype(BF16)
    rows = hot(iota((512, HID), 0) % HID == iota((512, HID), 1))
    cols = hot(iota((CH, 128), 1) % CH == iota((CH, 128), 0))
    full = mm(mm(rows, out_ref[...], NT).astype(BF16), cols)
    keep = iota((512, 128), 0) // HID == iota((512, 128), 1) // CH
    w2_ref[...] = jnp.where(keep, full, 0.0).astype(BF16)


def final_kernel(
    ids_ref, yi_ref, field_ref, tail_ref, iz_ref, in_ref, skip_ref, bias_ref, mout_ref, out_ref,
    y_ref, xa_ref, xb_ref, l_ref, w1_ref, w2_ref, b1_ref, *, ny, unroll
):
    expand_weights(in_ref, skip_ref, mout_ref, w1_ref, w2_ref)
    b1_ref[...] = jnp.concatenate([bias_ref[...]] * 8, 1)

    @pl.loop(0, 4)
    def _(kz):
        @pl.loop(0, 16, unroll=4)
        def _(s):
            for ri in range(2):
                at = pl.multiple_of(s * 128 + kz * 32 + ri * 16, 16)
                for p in range(2):
                    pair = split_lanes(
                        yi_ref[kz * 32 + s, ri, p].astype(F32),
                        yi_ref[kz * 32 + 16 + s, ri, p].astype(F32),
                    )
                    for e in range(2):
                        y_ref[2 * p + e, pl.ds(at, 16), :] = pair[e]

    def stage(i, x_ref):
        base = i * ny
        bx = base // 16
        for p in range(ny // 2):
            y = (base + 2 * p) % 16
            rhs = jnp.concatenate(
                [y_ref[bx, pl.ds(y + e, 128, stride=16), :] for e in range(2)], 1
            ).astype(BF16)
            res = mm(iz_ref[...], rhs).astype(BF16)
            for e in range(2):
                at = (2 * p + e) * GRID
                x_ref[at : at + GRID, 0:128] = res[:, e * 128 : e * 128 + 128]
                x_ref[at : at + GRID, 128:256] = field_ref[base + 2 * p + e]

    def layer(i, x_ref):
        h = gelu(mm(x_ref[...], w1_ref[...]) + b1_ref[...])
        o = mm(h, w2_ref[...]).astype(BF16).astype(F32)
        l_ref[pl.ds(i * ny, ny)] = o.reshape(ny, GRID, 128)

    steps = 64 // ny
    stage(0, xa_ref)

    @pl.loop(0, steps // 2)
    def _(i):
        stage(2 * i + 1, xb_ref)
        layer(2 * i, xa_ref)
        stage(jnp.minimum(2 * i + 2, steps - 1), xa_ref)
        layer(2 * i + 1, xb_ref)

    @pl.loop(0, NBLK // unroll)
    def _(i):
        for u in range(unroll):
            d = i * unroll + u
            weights = tail_ref[d, 32:48, :].astype(F32)
            heads = tail_ref[d, 48:56, :].astype(F32)
            for j in range(2):
                head = heads[4 * j : 4 * j + 4]
                basis = yz_basis(weights[8 * j : 8 * j + 8], head)
                b = ids_ref[2 * d + j]
                q = b // 32
                at = pl.multiple_of((b % 32) * 8, 8)
                cells = l_ref[pl.ds(q * 8, 8), pl.ds(at, 8), :].reshape(64, 128).astype(BF16)
                res = mm(cells, basis, TN)
                vx = jnp.broadcast_to(head[0:1, :], (16, NPTS))
                val = jnp.zeros((16, NPTS), F32)
                for x in range(7):
                    got = (
                        res[x * 16 : x * 16 + 16, 0:128]
                        + res[x * 16 + 16 : x * 16 + 32, 128:256]
                    )
                    val = jnp.where(vx == float(x), got, val)
                out_ref[2 * d + j] = val.astype(BF16)


def final(ids, yi, field, recv, iz, first, skip, bias, mout):
    smem = pl.BlockSpec(memory_space=pltpu.SMEM)
    vmem = pl.BlockSpec(memory_space=pltpu.VMEM)
    ny, unroll = 8, 16
    return pl.pallas_call(
        partial(final_kernel, ny=ny, unroll=unroll),
        out_shape=pltpu.VMEM((NSLOT, 16, NPTS), BF16),
        in_specs=[smem, vmem, vmem, vmem, vmem, vmem, vmem, vmem, vmem],
        out_specs=vmem,
        scratch_shapes=[
            pltpu.VMEM((4, 2048, 128), F32),
            pltpu.VMEM((ny * GRID, 256), BF16),
            pltpu.VMEM((ny * GRID, 256), BF16),
            pltpu.VMEM((64, GRID, 128), F32),
            pltpu.VMEM((256, 512), BF16),
            pltpu.VMEM((512, 128), BF16),
            pltpu.VMEM((1, 512), F32),
        ],
        compiler_params=grant(40),
        name="mlp_gather",
    )(ids, yi, field, recv, iz, first, skip, bias, mout)


def unpack_kernel(slot_ref, in_ref, out_ref):
    @pl.loop(0, NBLK, unroll=8)
    def _(b):
        at = pl.multiple_of(b * NPTS, NPTS)
        out_ref[:, pl.ds(at, NPTS)] = in_ref[slot_ref[b]]


def unpack(slots, vals):
    smem = pl.BlockSpec(memory_space=pltpu.SMEM)
    vmem = pl.BlockSpec(memory_space=pltpu.VMEM)
    return pl.pallas_call(
        unpack_kernel,
        out_shape=jax.ShapeDtypeStruct((CH, NBLK * NPTS), BF16),
        in_specs=[smem, vmem],
        out_specs=vmem,
        compiler_params=grant(16),
        name="unpack",
    )(slots, vals)


def a2a(x, axes):
    return lax.all_to_all(x, axes, split_axis=0, concat_axis=0, tiled=True)


def partner(x):
    return near(lax.ppermute(x, "row", [(i, i ^ 1) for i in range(ROWS)]))


def body(
    features,
    point_weights,
    point_corner,
    block_owner,
    block_cell,
    spec_weight,
    skip_weight,
    mlp_in,
    mlp_bias,
    mlp_out,
):
    tz, ty, tx, ix, iy, iz = tables()
    owner = block_owner.reshape(NBLK)
    row = lax.axis_index("row").astype(jnp.int32)[None]
    spec_weight = pltpu.with_memory_space_constraint(spec_weight, pltpu.HBM)
    corner = point_corner.reshape(NBLK, NPTS)
    send, slots, *parts = pack(
        row, owner, block_cell, features, point_weights, corner, spec_weight
    )
    parts = [
        near(lax.ppermute(part, "row", [(i, (i + 2 * d) % ROWS) for i in range(ROWS)]))
        for d, part in zip((1, 2, 3), parts)
    ]
    recv = near(a2a(send, ("row", "col")))
    field, zs, ids = scatter(recv, tz)
    zs = near(a2a(zs.reshape(128, 2, 2, 16, 128), ("row", "col")))
    keep, send = yx_forward(row, zs, ty, tx)
    keep, send = mix(row, keep, partner(send), spec_weight, parts)
    yi = near(a2a(xy_inverse(row, keep, partner(send), ix, iy), ("row", "col")))
    vals = final(
        ids, yi, field, recv, iz, mlp_in.T, skip_weight, mlp_bias.reshape(1, HID), mlp_out
    )
    return unpack(slots, near(a2a(vals, ("row", "col"))))


def solution(mesh):
    return jax.shard_map(
        body,
        mesh=mesh,
        in_specs=(
            P(None, ("row", "col")),
            P(None, ("row", "col")),
            P(("row", "col")),
            P(("row", "col"), None),
            P(("row", "col")),
            P("col", "row", None, None, None),
            P(),
            P(),
            P(),
            P(),
        ),
        out_specs=P(None, ("row", "col")),
        check_vma=False,
    )
```
